512 devices in a mesh: task: 32 (over z, core), tp: 16 (over y, x).
Axes of the slice: x: 4, y: 4, z: 16, core: 2. Of those that a mesh axis runs over, the one named last changes fastest.
Arguments:
- support_x: bfloat16 [32, 384, 3584], P('task'), may hold values from -6 to 6
- adapter_a: bfloat16 [32, 3584, 64], P('task'), may hold values from -0.09375 to 0.09375
- gate_pre: bfloat16 [32, 384, 10240], P('task', None, 'tp'), may hold values from -6 to 6
- lengths: int32 [32], P('task'), may hold values from 128 to 384, as said below
- damping: float32 [32], P('task'), may hold values from 0.03 to 0.3
- down_w: bfloat16 [10240, 3584], P('tp', 'task'), may hold values from -0.0625 to 0.0625
- grad_b: float32 [32, 64, 10240], P('task', None, 'tp'), may hold values from -6 to 6
Outputs:
- solution: float32 [32, 64, 10240], P('task', None, 'tp')
- residual: float32 [32, 64, 10240], P('task', None, 'tp')
The draws below stay inside these ranges and needn't reach their ends.
Inputs may be any that keep to these rules, and one draw needn't show every extreme that they name: `lengths`: each a multiple of 128; some task has exactly 384.
All inputs are finite; a program needn't handle non-finite values.
Results may differ from the reference program's by a relative error of at most 0.033.
Values may be sent and summed in bfloat16 or wider, within the bound.
No kernel may reach another device: no remote copies, remote signals or barrier semaphores. Data moves between devices by JAX's collectives and lax.ppermute only.
A program may use at most 64 MiB of HBM per device.

```python
import math
import jax
import jax.numpy as jnp
from jax import lax

D = 3584
FF_WIN = 10240
RANK = 64
BLOCK = 128
LEN = 384
ITERS = 2
TASKS = 32
N_TP = 16


def draw_lengths(key, part):
    blocks = jax.random.randint(key, (TASKS,), 1, LEN // BLOCK + 1)
    chosen = jax.random.randint(jax.random.fold_in(key, 7), (), 0, TASKS)
    blocks = jnp.where(jnp.arange(TASKS) == chosen, LEN // BLOCK, blocks)
    return (blocks * BLOCK).astype(jnp.int32)


def shard_levels(key, extent, split, low, top_value):
    loudness, own = 1.0, jax.random.fold_in(key, 6)
    for dim, shards_of in split:
        draws = jnp.exp(jax.random.uniform(jax.random.fold_in(own, dim), (shards_of,), jnp.float32, low / len(split), top_value / len(split)))
        loudness = loudness * jnp.repeat(draws, extent[dim] // shards_of).reshape([-1 if axis == dim else 1 for axis in range(len(extent))])
    return loudness


def gaussian(rng, shape, scale, reach, pieces=(), kind=jnp.bfloat16):
    values = scale * jax.random.normal(rng, shape, jnp.float32)
    if pieces:
        values = values * shard_levels(rng, shape, pieces, -0.22, 0.18)
    return jnp.clip(values, -reach, reach).astype(kind)


def setup_inputs(seed: int = 0) -> dict:
    streams_of = jax.random.split(jax.random.key(seed), 8)
    support_x = gaussian(streams_of[0], (TASKS, LEN, D), 1.0, 6.0, ((0, 32),))
    adapter_a = gaussian(streams_of[1], (TASKS, D, RANK), D ** -0.5, 0.09375, ((0, 32),))
    gate_pre = gaussian(streams_of[2], (TASKS, LEN, FF_WIN), 1.0, 6.0, ((0, 32), (2, 16)))
    lengths = draw_lengths(jax.random.fold_in(streams_of[7], 71), 0)
    damping = jnp.clip(jnp.exp(math.log(0.3) - 2.3025852 * jax.random.uniform(streams_of[4], (TASKS,), jnp.float32) ** shard_levels(streams_of[4], (TASKS,), ((0, 32),), -0.2, 0.2)), 0.03, 0.3)
    down_w = gaussian(streams_of[5], (FF_WIN, D), FF_WIN ** -0.5, 0.0625, ((0, 16), (1, 32)))
    grad_b = gaussian(streams_of[6], (TASKS, RANK, FF_WIN), 1.0, 6.0, ((0, 32), (2, 16)), jnp.float32)
    return dict(support_x=support_x, adapter_a=adapter_a, gate_pre=gate_pre, lengths=lengths, damping=damping, down_w=down_w, grad_b=grad_b)


def solve_task(operands, down_w):
    support, adapter, gate, length, damping_rate, target = operands
    width = FF_WIN // N_TP
    features = jnp.dot(support, adapter, preferred_element_type=jnp.float32).astype(jnp.bfloat16)
    positions = jnp.arange(LEN, dtype=jnp.int32)[:, None]
    gated = jnp.where(positions < length, jax.nn.silu(gate.astype(jnp.float32)), 0.0).astype(jnp.bfloat16)
    tokens_live = length.astype(jnp.float32)
    weights = down_w.reshape(N_TP, width, D).astype(jnp.float32)

    def apply(vector):
        inner = jnp.dot(features, vector.astype(jnp.bfloat16), preferred_element_type=jnp.float32)
        active = (gated.astype(jnp.float32) * inner).astype(jnp.bfloat16)
        grouped = active.reshape(LEN, N_TP, width).astype(jnp.float32)
        partial_sums = jnp.einsum("lgf,gfd->lgd", grouped, weights)
        rounded = lax.optimization_barrier(partial_sums.astype(jnp.bfloat16))
        mixed = jnp.sum(rounded.astype(jnp.float32), axis=1).astype(jnp.bfloat16)
        back = jnp.dot(mixed, down_w.T, preferred_element_type=jnp.float32)
        second = (gated.astype(jnp.float32) * back).astype(jnp.bfloat16)
        return jnp.dot(features.T, second, preferred_element_type=jnp.float32) / tokens_live + damping_rate * vector

    solution = jnp.zeros_like(target)
    residual = target
    direction = target
    norm_now = jnp.sum(residual * residual)
    for step in range(ITERS):
        image = apply(direction)
        alpha = norm_now / jnp.sum(direction * image)
        solution = solution + alpha * direction
        residual = residual - alpha * image
        norm_next = jnp.sum(residual * residual)
        direction = residual + (norm_next / norm_now) * direction
        norm_now = norm_next
    return solution, residual


def reference(support_x, adapter_a, gate_pre, lengths, damping, down_w, grad_b):
    def per_task(operands):
        return solve_task(operands, down_w)

    return lax.map(per_task, (support_x, adapter_a, gate_pre, lengths, damping, grad_b))
```

```python
import functools

import jax
import jax.numpy as jnp
from jax import lax
from jax.experimental import pallas as pl
from jax.experimental.pallas import tpu as pltpu
from jax.sharding import Mesh
from jax.sharding import PartitionSpec as P

F32, BF16 = jnp.float32, jnp.bfloat16
HALF = ("y", "xb")
ROW = ("xa", "xb")
ALL = ("y", "xa", "xb")
EXTRA = 8
TAIL = 16
VMEM_LIMIT = 48 << 20


def product(a, b, dims):
    return lax.dot_general(a, b, (dims, ((), ())), preferred_element_type=F32)


def in_pieces(values, shape):
    row = lax.broadcasted_iota(jnp.int32, shape, 0)
    out, at = jnp.zeros(shape, F32), 0
    for value in values:
        rest = jnp.broadcast_to(value, shape)
        for _ in range(3):
            piece = rest.astype(BF16).astype(F32)
            out = jnp.where(row == at, piece, out)
            rest = rest - piece
            at += 1
    return out.astype(BF16)


def from_pieces(rows, at):
    return rows[at : at + 1] + rows[at + 1 : at + 2] + rows[at + 2 : at + 3]


def everywhere(value, shape):
    return jnp.broadcast_to(value[:, :1], shape)


def total(array):
    return jnp.sum(jnp.sum(array, axis=0, keepdims=True), axis=1, keepdims=True)


def post(message, body, scalars, rank):
    pieces = in_pieces(scalars, (EXTRA, body.shape[1]))
    for j in range(message.shape[0]):
        message[j, :rank, :] = body
        message[j, rank:, :] = pieces


def first_message(grad, message):
    g = grad[...]
    post(message, g.astype(BF16), [total(g * g)], g.shape[0])


def forward(rank, features, gated, vectors, weights, partial, acc, scalars):
    step = pl.program_id(0)
    tokens = features.shape[0]

    @pl.when(step == 0)
    def _():
        acc[...] = jnp.zeros_like(acc)
        scalars[...] = jnp.zeros_like(scalars)

    inner = product(features[...], vectors[0, :rank, :], ((1,), (0,)))
    active = (gated[0].astype(F32) * inner).astype(BF16)
    acc[...] += product(active, weights[...], ((1,), (1,)))
    scalars[...] += vectors[0, rank:, : scalars.shape[1]].astype(F32)

    @pl.when(step == pl.num_programs(0) - 1)
    def _():
        partial[:tokens, :] = acc[...].astype(BF16)
        rows = scalars[...]
        partial[tokens:, :] = in_pieces(
            [from_pieces(rows, 0), from_pieces(rows, 3)], (TAIL, rows.shape[1])
        )


def summed(own, other, tokens):
    mixed = own[:tokens, :].astype(F32) + other[:tokens, :].astype(F32)
    return mixed, own[tokens:, :].astype(F32) + other[tokens:, :].astype(F32)


def backward(rank, second_pass, *refs):
    if second_pass:
        features, gated, own, other, own_was, other_was, weights, message, mixed, norm = refs
    else:
        features, gated, own, other, weights, message, mixed, norm = refs
    step = pl.program_id(0)
    tokens = features.shape[0]

    @pl.when(step == 0)
    def _():
        value, rows = summed(own, other, tokens)
        if second_pass:
            before, rows_before = summed(own_was, other_was, tokens)
            ratio = from_pieces(rows, 0) / from_pieces(rows_before, 0)
            value = value + everywhere(ratio, value.shape) * before
        rounded = value.astype(BF16)
        mixed[...] = rounded
        norm[...] = jnp.broadcast_to(total(value * rounded.astype(F32)), norm.shape)

    back = product(mixed[...], weights[...], ((1,), (0,)))
    second = (gated[0].astype(F32) * back).astype(BF16)
    message[0, :rank, :] = product(features[...], second, ((0,), (0,))).astype(BF16)
    message[0, rank:, :] = in_pieces([norm[:1, :1]], (EXTRA, second.shape[1]))


def update(rank, live, rate, arrived, grad, own, other, message, residual, alpha):
    rows = arrived[0].astype(F32)
    for j in range(1, arrived.shape[0]):
        rows = rows + arrived[j].astype(F32)
    g = grad[...]
    tail = own[...].astype(F32) + other[...].astype(F32)
    shape = (1, g.shape[1])
    norm = everywhere(from_pieces(tail, 0), shape)
    step = norm / (from_pieces(rows[rank:], 0) / live[0] + rate[0] * norm)
    h = rows[:rank] / live[0] + rate[0] * g
    r = g - step * h
    residual[...] = r
    alpha[...] = jnp.broadcast_to(step, alpha.shape)
    post(message, r.astype(BF16), [total(r * r), total(r * g)], rank)


def finish(rank, live, rate, arrived, grad, own, other, own_was, other_was, residual, alpha, x, left):
    rows = arrived[0].astype(F32)
    for j in range(1, arrived.shape[0]):
        rows = rows + arrived[j].astype(F32)
    g, r = grad[...], residual[...]
    shape = (1, g.shape[1])
    tail = own[...].astype(F32) + other[...].astype(F32)
    tail_was = own_was[...].astype(F32) + other_was[...].astype(F32)
    norm = everywhere(from_pieces(tail, 0), shape)
    cross = everywhere(from_pieces(tail, 3), shape)
    norm_was = everywhere(from_pieces(tail_was, 0), shape)
    ratio = norm / norm_was
    length = norm + ratio * (2.0 * cross + ratio * norm_was)
    step = norm / (from_pieces(rows[rank:], 0) / live[0] + rate[0] * length)
    d = r + ratio * g
    h = rows[:rank] / live[0] + rate[0] * d
    x[...] = alpha[:1, :] * g + step * d
    left[...] = r - step * h


def whole(array_shape):
    return pl.BlockSpec(array_shape, lambda *_: (0,) * len(array_shape))


SCALAR = pl.BlockSpec(memory_space=pltpu.SMEM)


def params():
    return pltpu.CompilerParams(vmem_limit_bytes=VMEM_LIMIT)


def swapped(array):
    return lax.ppermute(array, ROW, [(0, 3), (3, 0), (1, 2), (2, 1)])


def exchanged(array):
    return lax.all_to_all(array, HALF, split_axis=0, concat_axis=0, tiled=True)


def width_block(down_w):
    members = lax.axis_size(HALF)
    units, columns = down_w.shape
    share = columns // members
    padded = -(-share // 16) * 16
    pieces = down_w.T.reshape(members // 2, 2, share, units)
    pieces = jnp.where(lax.axis_index("xa") == 1, pieces[:, ::-1], pieces)
    pieces = jnp.pad(pieces.reshape(members, share, units), ((0, 0), (0, padded - share), (0, 0)))
    mine = exchanged(pieces)
    mine = jnp.swapaxes(mine, 0, 1).reshape(padded, members * units)
    return lax.all_gather(mine, "task", axis=0, tiled=True)


def shards(support_x, adapter_a, gate_pre, lengths, damping, down_w, grad_b):
    members = lax.axis_size(HALF)
    tokens, units = gate_pre.shape[1:]
    rank = adapter_a.shape[2]
    target = grad_b[0]
    rows = rank + EXTRA
    block_message = pl.BlockSpec((1, rows, units), lambda i: (i, 0, 0))
    block_gated = pl.BlockSpec((1, tokens, units), lambda i: (i, 0, 0))
    message_shape = jax.ShapeDtypeStruct((members, rows, units), BF16)
    state = jax.ShapeDtypeStruct((rank, units), F32)

    weights = width_block(down_w)
    width = weights.shape[0]
    block_weights = pl.BlockSpec((width, units), lambda i: (0, i))

    vectors = exchanged(pl.pallas_call(first_message, out_shape=message_shape)(target))
    positions = lax.broadcasted_iota(jnp.int32, (tokens, 1), 0)
    gated = jnp.where(
        positions < lengths[0], jax.nn.silu(gate_pre[0].astype(F32)), 0.0
    ).astype(BF16)
    gated = exchanged(jnp.broadcast_to(gated, (members, tokens, units)))
    features = jnp.dot(support_x[0], adapter_a[0], preferred_element_type=F32).astype(BF16)
    live = lengths.astype(F32)
    flops = 2 * tokens * units * members * (width + rank)
    moved = 2 * units * members * (tokens + width + rows)

    cost = pl.CostEstimate(flops=flops, bytes_accessed=moved, transcendentals=0)

    partial_shape = (tokens + TAIL, width)

    def mixed_shares(vectors):
        own = pl.pallas_call(
            functools.partial(forward, rank),
            grid=(members,),
            in_specs=[whole((tokens, rank)), block_gated, block_message, block_weights],
            out_specs=whole(partial_shape),
            out_shape=jax.ShapeDtypeStruct(partial_shape, BF16),
            scratch_shapes=[pltpu.VMEM((tokens, width), F32), pltpu.VMEM((EXTRA, width), F32)],
            compiler_params=params(),
            cost_estimate=cost,
        )(features, gated, vectors, weights)
        return own, swapped(own)

    def product_shares(*shares):
        return exchanged(
            pl.pallas_call(
                functools.partial(backward, rank, len(shares) == 4),
                grid=(members,),
                in_specs=[whole((tokens, rank)), block_gated]
                + [whole(partial_shape)] * len(shares)
                + [block_weights],
                out_specs=block_message,
                out_shape=message_shape,
                scratch_shapes=[pltpu.VMEM((tokens, width), BF16), pltpu.VMEM((8, 128), F32)],
                compiler_params=params(),
                cost_estimate=cost,
            )(features, gated, *shares, weights)
        )

    tail = pl.BlockSpec((TAIL, width), lambda i: (tokens // TAIL, 0))
    full_message = whole(message_shape.shape)
    full_state = whole(state.shape)
    full_alpha = whole((8, units))

    first = mixed_shares(vectors)
    arrived = product_shares(*first)
    message, residual, alpha = pl.pallas_call(
        functools.partial(update, rank),
        grid=(1,),
        in_specs=[SCALAR, SCALAR, full_message, full_state, tail, tail],
        out_specs=[full_message, full_state, full_alpha],
        out_shape=[message_shape, state, jax.ShapeDtypeStruct((8, units), F32)],
        compiler_params=params(),
    )(live, damping, arrived, target, *first)
    second = mixed_shares(exchanged(message))
    arrived = product_shares(*second, *first)
    x, left = pl.pallas_call(
        functools.partial(finish, rank),
        grid=(1,),
        in_specs=[SCALAR, SCALAR, full_message, full_state] + [tail] * 4 + [full_state, full_alpha],
        out_specs=[full_state, full_state],
        out_shape=[state, state],
        compiler_params=params(),
    )(live, damping, arrived, target, *second, *first, residual, alpha)
    return (x[None], left[None])


def solution(mesh):
    split = Mesh(mesh.devices.reshape(mesh.shape["task"], 4, 2, 2), ("task", "y", "xa", "xb"))
    return jax.shard_map(
        shards,
        mesh=split,
        in_specs=(
            P("task", None, None),
            P("task", None, None),
            P("task", None, ALL),
            P("task"),
            P("task"),
            P(ALL, "task"),
            P("task", None, ALL),
        ),
        out_specs=(P("task", None, ALL), P("task", None, ALL)),
        check_vma=False,
    )
```

```python
import functools

import jax
import jax.numpy as jnp
from jax import lax
from jax.experimental import pallas as pl
from jax.experimental.pallas import tpu as pltpu
from jax.sharding import Mesh
from jax.sharding import PartitionSpec as P

F32, BF16 = jnp.float32, jnp.bfloat16
HALF = ("y", "xb")
ROW = ("xa", "xb")
ALL = ("y", "xa", "xb")
EXTRA = 8
TAIL = 16
VMEM_LIMIT = 56 << 20
TOGETHER = 2


def product(a, b, dims):
    return lax.dot_general(a, b, (dims, ((), ())), preferred_element_type=F32)


def in_pieces(values, shape):
    row = lax.broadcasted_iota(jnp.int32, shape, 0)
    out, at = jnp.zeros(shape, F32), 0
    for value in values:
        rest = jnp.broadcast_to(value, shape)
        for _ in range(3):
            piece = rest.astype(BF16).astype(F32)
            out = jnp.where(row == at, piece, out)
            rest = rest - piece
            at += 1
    return out.astype(BF16)


def from_pieces(rows, at):
    return rows[at : at + 1] + rows[at + 1 : at + 2] + rows[at + 2 : at + 3]


def everywhere(value, shape):
    return jnp.broadcast_to(value[:, :1], shape)


def total(array):
    return jnp.sum(jnp.sum(array, axis=0, keepdims=True), axis=1, keepdims=True)


def post(message, body, scalars, rank):
    pieces = in_pieces(scalars, (EXTRA, body.shape[1]))
    for j in range(message.shape[0]):
        message[j, :rank, :] = body
        message[j, rank:, :] = pieces


def first_message(grad, message):
    g = grad[...]
    post(message, g.astype(BF16), [total(g * g)], g.shape[0])


def forward(rank, count, features, gated, vectors, *refs):
    pieces, (partial, *outs) = refs[:count], refs[count:]
    if count > 1:
        weights, active, acc, scalars = outs
        at = 0
        for piece in pieces:
            weights[at : at + piece.shape[0], :] = piece[...]
            at += piece.shape[0]
    else:
        (weights,), (active, acc, scalars) = pieces, outs
    step = pl.program_id(0)
    tokens = features.shape[0]
    units = gated.shape[2]

    @pl.when(step == 0)
    def _():
        acc[...] = jnp.zeros_like(acc)
        scalars[...] = jnp.zeros_like(scalars)

    for j in range(gated.shape[0]):
        inner = product(features[...], vectors[j, :rank, :], ((1,), (0,)))
        at = slice(j * units, (j + 1) * units)
        active[:, at] = (gated[j].astype(F32) * inner).astype(BF16)
        scalars[...] += vectors[j, rank:, : scalars.shape[1]].astype(F32)
    acc[...] += product(active[...], weights[...], ((1,), (1,)))

    @pl.when(step == pl.num_programs(0) - 1)
    def _():
        partial[:tokens, :] = acc[...].astype(BF16)
        rows = scalars[...]
        partial[tokens:, :] = in_pieces(
            [from_pieces(rows, 0), from_pieces(rows, 3)], (TAIL, rows.shape[1])
        )


def summed(own, other, tokens):
    mixed = own[:tokens, :].astype(F32) + other[:tokens, :].astype(F32)
    return mixed, own[tokens:, :].astype(F32) + other[tokens:, :].astype(F32)


def backward(rank, second_pass, *refs):
    if second_pass:
        features, gated, own, other, own_was, other_was, weights, message, mixed, norm = refs
    else:
        features, gated, own, other, weights, message, mixed, norm = refs
    step = pl.program_id(0)
    tokens = features.shape[0]

    @pl.when(step == 0)
    def _():
        value, rows = summed(own, other, tokens)
        if second_pass:
            before, rows_before = summed(own_was, other_was, tokens)
            ratio = from_pieces(rows, 0) / from_pieces(rows_before, 0)
            value = value + everywhere(ratio, value.shape) * before
        rounded = value.astype(BF16)
        mixed[...] = rounded
        norm[...] = jnp.broadcast_to(total(value * rounded.astype(F32)), norm.shape)

    units = gated.shape[2]
    pieces = in_pieces([norm[:1, :1]], (EXTRA, units))
    for j in range(gated.shape[0]):
        back = product(mixed[...], weights[:, j * units : (j + 1) * units], ((1,), (0,)))
        second = (gated[j].astype(F32) * back).astype(BF16)
        message[j, :rank, :] = product(features[...], second, ((0,), (0,))).astype(BF16)
        message[j, rank:, :] = pieces


def update(rank, live, rate, arrived, grad, own, other, message, residual, alpha):
    rows = arrived[0].astype(F32)
    for j in range(1, arrived.shape[0]):
        rows = rows + arrived[j].astype(F32)
    g = grad[...]
    tail = own[...].astype(F32) + other[...].astype(F32)
    shape = (1, g.shape[1])
    norm = everywhere(from_pieces(tail, 0), shape)
    step = norm / (from_pieces(rows[rank:], 0) / live[0] + rate[0] * norm)
    h = rows[:rank] / live[0] + rate[0] * g
    r = g - step * h
    residual[...] = r
    alpha[...] = jnp.broadcast_to(step, alpha.shape)
    post(message, r.astype(BF16), [total(r * r), total(r * g)], rank)


def finish(rank, live, rate, arrived, grad, own, other, own_was, other_was, residual, alpha, x, left):
    rows = arrived[0].astype(F32)
    for j in range(1, arrived.shape[0]):
        rows = rows + arrived[j].astype(F32)
    g, r = grad[...], residual[...]
    shape = (1, g.shape[1])
    tail = own[...].astype(F32) + other[...].astype(F32)
    tail_was = own_was[...].astype(F32) + other_was[...].astype(F32)
    norm = everywhere(from_pieces(tail, 0), shape)
    cross = everywhere(from_pieces(tail, 3), shape)
    norm_was = everywhere(from_pieces(tail_was, 0), shape)
    ratio = norm / norm_was
    length = norm + ratio * (2.0 * cross + ratio * norm_was)
    step = norm / (from_pieces(rows[rank:], 0) / live[0] + rate[0] * length)
    d = r + ratio * g
    h = rows[:rank] / live[0] + rate[0] * d
    x[...] = alpha[:1, :] * g + step * d
    left[...] = r - step * h


def whole(array_shape):
    return pl.BlockSpec(array_shape, lambda *_: (0,) * len(array_shape))


SCALAR = pl.BlockSpec(memory_space=pltpu.SMEM)


def params():
    return pltpu.CompilerParams(vmem_limit_bytes=VMEM_LIMIT)


def swapped(array):
    return lax.ppermute(array, ROW, [(0, 3), (3, 0), (1, 2), (2, 1)])


def exchanged(array):
    return lax.all_to_all(array, HALF, split_axis=0, concat_axis=0, tiled=True)


def shifted(array, by):
    size = lax.axis_size("z")
    return lax.ppermute(array, "z", [(i, (i + by) % size) for i in range(size)])


def other_core(array):
    return lax.ppermute(array, "c", [(0, 1), (1, 0)])


def width_block(down_w):
    members = lax.axis_size(HALF)
    units, columns = down_w.shape
    share = columns // members
    padded = -(-share // 16) * 16
    pieces = down_w.T.reshape(members // 2, 2, share, units)
    pieces = jnp.where(lax.axis_index("xa") == 1, pieces[:, ::-1], pieces)
    pieces = jnp.pad(pieces.reshape(members, share, units), ((0, 0), (0, padded - share), (0, 0)))
    mine = exchanged(pieces)
    return jnp.swapaxes(mine, 0, 1).reshape(padded, members * units)


def all_blocks(mine):
    rows = mine.shape[0]
    near = jnp.concatenate([mine, shifted(mine, 5), shifted(mine, -5)], axis=0)
    up, down = shifted(near, 1), shifted(near, -1)
    up2, down2 = shifted(up, 1), shifted(down, -1)
    half = rows // 2
    last = [shifted(up2[rows : rows + half], 1), shifted(down2[2 * rows + half :], -1)]
    pieces = [near, up, down, up2, down2, *last]
    return pieces + [other_core(piece) for piece in pieces]


def shards(support_x, adapter_a, gate_pre, lengths, damping, down_w, grad_b):
    members = lax.axis_size(HALF)
    tokens, units = gate_pre.shape[1:]
    rank = adapter_a.shape[2]
    target = grad_b[0]
    rows = rank + EXTRA
    block_message = pl.BlockSpec((TOGETHER, rows, units), lambda i: (i, 0, 0))
    block_gated = pl.BlockSpec((TOGETHER, tokens, units), lambda i: (i, 0, 0))
    span = TOGETHER * units
    steps = members // TOGETHER
    message_shape = jax.ShapeDtypeStruct((members, rows, units), BF16)
    state = jax.ShapeDtypeStruct((rank, units), F32)

    pieces = all_blocks(width_block(down_w))
    width = sum(piece.shape[0] for piece in pieces)

    def block_weights(array):
        return pl.BlockSpec((array.shape[0], span), lambda i: (0, i))

    vectors = exchanged(pl.pallas_call(first_message, out_shape=message_shape)(target))
    positions = lax.broadcasted_iota(jnp.int32, (tokens, 1), 0)
    gated = jnp.where(
        positions < lengths[0], jax.nn.silu(gate_pre[0].astype(F32)), 0.0
    ).astype(BF16)
    gated = exchanged(jnp.broadcast_to(gated, (members, tokens, units)))
    features = jnp.dot(support_x[0], adapter_a[0], preferred_element_type=F32).astype(BF16)
    live = lengths.astype(F32)
    flops = 2 * tokens * units * members * (width + rank)
    moved = 2 * units * members * (tokens + width + rows)

    cost = pl.CostEstimate(flops=flops, bytes_accessed=moved, transcendentals=0)

    partial_shape = (tokens + TAIL, width)

    def mixed_shares(vectors, pieces):
        shapes = [jax.ShapeDtypeStruct(partial_shape, BF16)]
        specs = [whole(partial_shape)]
        if len(pieces) > 1:
            shapes.append(jax.ShapeDtypeStruct((width, units * members), BF16))
            specs.append(block_weights(shapes[1]))
        own, *weights = pl.pallas_call(
            functools.partial(forward, rank, len(pieces)),
            grid=(steps,),
            in_specs=[whole((tokens, rank)), block_gated, block_message]
            + [block_weights(piece) for piece in pieces],
            out_specs=specs,
            out_shape=shapes,
            scratch_shapes=[
                pltpu.VMEM((tokens, span), BF16),
                pltpu.VMEM((tokens, width), F32),
                pltpu.VMEM((EXTRA, width), F32),
            ],
            compiler_params=params(),
            cost_estimate=cost,
        )(features, gated, vectors, *pieces)
        return (own, swapped(own)), weights

    def product_shares(weights, *shares):
        return exchanged(
            pl.pallas_call(
                functools.partial(backward, rank, len(shares) == 4),
                grid=(steps,),
                in_specs=[whole((tokens, rank)), block_gated]
                + [whole(partial_shape)] * len(shares)
                + [block_weights(weights)],
                out_specs=block_message,
                out_shape=message_shape,
                scratch_shapes=[pltpu.VMEM((tokens, width), BF16), pltpu.VMEM((8, 128), F32)],
                compiler_params=params(),
                cost_estimate=cost,
            )(features, gated, *shares, weights)
        )

    tail = pl.BlockSpec((TAIL, width), lambda i: (tokens // TAIL, 0))
    full_message = whole(message_shape.shape)
    full_state = whole(state.shape)
    full_alpha = whole((8, units))

    first, (weights,) = mixed_shares(vectors, pieces)
    arrived = product_shares(weights, *first)
    message, residual, alpha = pl.pallas_call(
        functools.partial(update, rank),
        grid=(1,),
        in_specs=[SCALAR, SCALAR, full_message, full_state, tail, tail],
        out_specs=[full_message, full_state, full_alpha],
        out_shape=[message_shape, state, jax.ShapeDtypeStruct((8, units), F32)],
        compiler_params=params(),
    )(live, damping, arrived, target, *first)
    second, _ = mixed_shares(exchanged(message), [weights])
    arrived = product_shares(weights, *second, *first)
    x, left = pl.pallas_call(
        functools.partial(finish, rank),
        grid=(1,),
        in_specs=[SCALAR, SCALAR, full_message, full_state] + [tail] * 4 + [full_state, full_alpha],
        out_specs=[full_state, full_state],
        out_shape=[state, state],
        compiler_params=params(),
    )(live, damping, arrived, target, *second, *first, residual, alpha)
    return (x[None], left[None])


def solution(mesh):
    tasks = mesh.shape["task"]
    split = Mesh(mesh.devices.reshape(tasks // 2, 2, 4, 2, 2), ("z", "c", "y", "xa", "xb"))
    task = ("z", "c")
    return jax.shard_map(
        shards,
        mesh=split,
        in_specs=(
            P(task, None, None),
            P(task, None, None),
            P(task, None, ALL),
            P(task),
            P(task),
            P(ALL, task),
            P(task, None, ALL),
        ),
        out_specs=(P(task, None, ALL), P(task, None, ALL)),
        check_vma=False,
    )
```

```python
import functools

import jax
import jax.numpy as jnp
from jax import lax
from jax.experimental import pallas as pl
from jax.experimental.pallas import tpu as pltpu
from jax.sharding import Mesh
from jax.sharding import PartitionSpec as P

F32, BF16 = jnp.float32, jnp.bfloat16
HALF = ("y", "xb")
ROW = ("xa", "xb")
ALL = ("y", "xa", "xb")
EXTRA = 8
TAIL = 16
VMEM_LIMIT = 56 << 20
TOGETHER = 2


def product(a, b, dims):
    return lax.dot_general(a, b, (dims, ((), ())), preferred_element_type=F32)


def in_pieces(values, shape):
    row = lax.broadcasted_iota(jnp.int32, shape, 0)
    out, at = jnp.zeros(shape, F32), 0
    for value in values:
        rest = jnp.broadcast_to(value, shape)
        for _ in range(3):
            piece = rest.astype(BF16).astype(F32)
            out = jnp.where(row == at, piece, out)
            rest = rest - piece
            at += 1
    return out.astype(BF16)


def from_pieces(rows, at):
    return rows[at : at + 1] + rows[at + 1 : at + 2] + rows[at + 2 : at + 3]


def everywhere(value, shape):
    return jnp.broadcast_to(value[:, :1], shape)


def total(array):
    return jnp.sum(jnp.sum(array, axis=0, keepdims=True), axis=1, keepdims=True)


def post(message, body, scalars, rank):
    pieces = in_pieces(scalars, (EXTRA, body.shape[1]))
    for j in range(message.shape[0]):
        message[j, :rank, :] = body
        message[j, rank:, :] = pieces


def pack(live, gate, grad, message, held):
    tokens = gate.shape[0]
    rank = grad.shape[0]

    @pl.when(pl.program_id(0) == 0)
    def _():
        v = gate[...].astype(F32)
        row = lax.broadcasted_iota(jnp.int32, v.shape, 0)
        held[:tokens, :] = jnp.where(row < live[0], v / (1.0 + jnp.exp(-v)), 0.0).astype(BF16)
        g = grad[...]
        held[tokens : tokens + rank, :] = g.astype(BF16)
        held[tokens + rank :, :] = in_pieces([total(g * g)], (held.shape[0] - tokens - rank, g.shape[1]))

    message[0] = held[...]


def forward(rank, count, features, gated, vectors, *refs):
    pieces, (partial, *outs) = refs[:count], refs[count:]
    if count > 1:
        weights, active, acc, scalars = outs
        at = 0
        for piece in pieces:
            weights[at : at + piece.shape[0], :] = piece[...]
            at += piece.shape[0]
    else:
        (weights,), (active, acc, scalars) = pieces, outs
    step = pl.program_id(0)
    tokens = features.shape[0]
    units = gated.shape[2]

    @pl.when(step == 0)
    def _():
        acc[...] = jnp.zeros_like(acc)
        scalars[...] = jnp.zeros_like(scalars)

    for j in range(gated.shape[0]):
        inner = product(features[...], vectors[j, :rank, :], ((1,), (0,)))
        at = slice(j * units, (j + 1) * units)
        active[:, at] = (gated[j].astype(F32) * inner).astype(BF16)
        scalars[...] += vectors[j, rank : rank + EXTRA, : scalars.shape[1]].astype(F32)
    acc[...] += product(active[...], weights[...], ((1,), (1,)))

    @pl.when(step == pl.num_programs(0) - 1)
    def _():
        partial[:tokens, :] = acc[...].astype(BF16)
        rows = scalars[...]
        partial[tokens:, :] = in_pieces(
            [from_pieces(rows, 0), from_pieces(rows, 3)], (TAIL, rows.shape[1])
        )


def summed(own, other, tokens):
    mixed = own[:tokens, :].astype(F32) + other[:tokens, :].astype(F32)
    return mixed, own[tokens:, :].astype(F32) + other[tokens:, :].astype(F32)


def backward(rank, second_pass, *refs):
    if second_pass:
        features, gated, own, other, own_was, other_was, weights, message, mixed, norm = refs
    else:
        features, gated, own, other, weights, message, mixed, norm = refs
    step = pl.program_id(0)
    tokens = features.shape[0]

    @pl.when(step == 0)
    def _():
        value, rows = summed(own, other, tokens)
        if second_pass:
            before, rows_before = summed(own_was, other_was, tokens)
            ratio = from_pieces(rows, 0) / from_pieces(rows_before, 0)
            value = value + everywhere(ratio, value.shape) * before
        rounded = value.astype(BF16)
        mixed[...] = rounded
        norm[...] = jnp.broadcast_to(total(value * rounded.astype(F32)), norm.shape)

    units = gated.shape[2]
    pieces = in_pieces([norm[:1, :1]], (EXTRA, units))
    for j in range(gated.shape[0]):
        back = product(mixed[...], weights[:, j * units : (j + 1) * units], ((1,), (0,)))
        second = (gated[j].astype(F32) * back).astype(BF16)
        message[j, :rank, :] = product(features[...], second, ((0,), (0,))).astype(BF16)
        message[j, rank:, :] = pieces


def update(rank, live, rate, arrived, grad, own, other, message, residual, alpha):
    rows = arrived[0].astype(F32)
    for j in range(1, arrived.shape[0]):
        rows = rows + arrived[j].astype(F32)
    g = grad[...]
    tail = own[...].astype(F32) + other[...].astype(F32)
    shape = (1, g.shape[1])
    norm = everywhere(from_pieces(tail, 0), shape)
    step = norm / (from_pieces(rows[rank:], 0) / live[0] + rate[0] * norm)
    h = rows[:rank] / live[0] + rate[0] * g
    r = g - step * h
    residual[...] = r
    alpha[...] = jnp.broadcast_to(step, alpha.shape)
    post(message, r.astype(BF16), [total(r * r), total(r * g)], rank)


def finish(rank, live, rate, arrived, grad, own, other, own_was, other_was, residual, alpha, x, left):
    rows = arrived[0].astype(F32)
    for j in range(1, arrived.shape[0]):
        rows = rows + arrived[j].astype(F32)
    g, r = grad[...], residual[...]
    shape = (1, g.shape[1])
    tail = own[...].astype(F32) + other[...].astype(F32)
    tail_was = own_was[...].astype(F32) + other_was[...].astype(F32)
    norm = everywhere(from_pieces(tail, 0), shape)
    cross = everywhere(from_pieces(tail, 3), shape)
    norm_was = everywhere(from_pieces(tail_was, 0), shape)
    ratio = norm / norm_was
    length = norm + ratio * (2.0 * cross + ratio * norm_was)
    step = norm / (from_pieces(rows[rank:], 0) / live[0] + rate[0] * length)
    d = r + ratio * g
    h = rows[:rank] / live[0] + rate[0] * d
    x[...] = alpha[:1, :] * g + step * d
    left[...] = r - step * h


def whole(array_shape):
    return pl.BlockSpec(array_shape, lambda *_: (0,) * len(array_shape))


SCALAR = pl.BlockSpec(memory_space=pltpu.SMEM)


def params():
    return pltpu.CompilerParams(vmem_limit_bytes=VMEM_LIMIT)


def swapped(array):
    return lax.ppermute(array, ROW, [(0, 3), (3, 0), (1, 2), (2, 1)])


def exchanged(array):
    return lax.all_to_all(array, HALF, split_axis=0, concat_axis=0, tiled=True)


def shifted(array, by):
    size = lax.axis_size("z")
    return lax.ppermute(array, "z", [(i, (i + by) % size) for i in range(size)])


def other_core(array):
    return lax.ppermute(array, "c", [(0, 1), (1, 0)])


def width_block(down_w):
    members = lax.axis_size(HALF)
    units, columns = down_w.shape
    share = columns // members
    padded = -(-share // 16) * 16
    pieces = down_w.T.reshape(members // 2, 2, share, units)
    pieces = jnp.where(lax.axis_index("xa") == 1, pieces[:, ::-1], pieces)
    pieces = jnp.pad(pieces.reshape(members, share, units), ((0, 0), (0, padded - share), (0, 0)))
    mine = exchanged(pieces)
    return jnp.swapaxes(mine, 0, 1).reshape(padded, members * units)


def start_blocks(mine):
    return jnp.concatenate([mine, shifted(mine, 5), shifted(mine, -5)], axis=0)


def all_blocks(near):
    rows = near.shape[0] // 3
    up, down = shifted(near, 1), shifted(near, -1)
    up2, down2 = shifted(up, 1), shifted(down, -1)
    far = jnp.where(lax.axis_index("c") == 0, up2[rows : 2 * rows], down2[2 * rows :])
    size = lax.axis_size("z")
    both_ways = [(2 * i, 2 * ((i + 1) % size)) for i in range(size)]
    both_ways += [(2 * i + 1, 2 * ((i - 1) % size) + 1) for i in range(size)]
    last = lax.ppermute(far, ("z", "c"), both_ways)
    pieces = [near, up, down, up2, down2, last]
    return pieces + [other_core(piece) for piece in pieces]


def shards(support_x, adapter_a, gate_pre, lengths, damping, down_w, grad_b):
    members = lax.axis_size(HALF)
    tokens, units = gate_pre.shape[1:]
    rank = adapter_a.shape[2]
    target = grad_b[0]
    rows = rank + EXTRA
    block_message = pl.BlockSpec((TOGETHER, rows, units), lambda i: (i, 0, 0))
    block_gated = pl.BlockSpec((TOGETHER, tokens, units), lambda i: (i, 0, 0))
    span = TOGETHER * units
    steps = members // TOGETHER
    message_shape = jax.ShapeDtypeStruct((members, rows, units), BF16)
    state = jax.ShapeDtypeStruct((rank, units), F32)

    first_rows = rank + 4 * EXTRA
    packed_shape = (tokens + first_rows, units)
    packed = pl.pallas_call(
        pack,
        grid=(members,),
        in_specs=[SCALAR, whole((tokens, units)), whole((rank, units))],
        out_specs=pl.BlockSpec((1, *packed_shape), lambda i: (i, 0, 0)),
        out_shape=jax.ShapeDtypeStruct((members, *packed_shape), BF16),
        scratch_shapes=[pltpu.VMEM(packed_shape, BF16)],
        compiler_params=params(),
        cost_estimate=pl.CostEstimate(
            flops=8 * tokens * units,
            bytes_accessed=2 * members * packed_shape[0] * units,
            transcendentals=tokens * units,
        ),
    )(lengths, gate_pre[0], target)
    block_first = pl.BlockSpec((TOGETHER, first_rows, units), lambda i: (i, tokens // first_rows, 0))
    mine = width_block(down_w)
    mine, packed = lax.optimization_barrier((mine, packed))
    gated = exchanged(packed)
    features = jnp.dot(support_x[0], adapter_a[0], preferred_element_type=F32).astype(BF16)
    near, features = lax.optimization_barrier((start_blocks(mine), features))
    pieces = all_blocks(near)
    width = sum(piece.shape[0] for piece in pieces)

    def block_weights(array):
        return pl.BlockSpec((array.shape[0], span), lambda i: (0, i))

    live = lengths.astype(F32)
    flops = 2 * tokens * units * members * (width + rank)
    moved = 2 * units * members * (tokens + width + rows)

    cost = pl.CostEstimate(flops=flops, bytes_accessed=moved, transcendentals=0)

    partial_shape = (tokens + TAIL, width)

    def mixed_shares(vectors, pieces):
        shapes = [jax.ShapeDtypeStruct(partial_shape, BF16)]
        specs = [whole(partial_shape)]
        if len(pieces) > 1:
            shapes.append(jax.ShapeDtypeStruct((width, units * members), BF16))
            specs.append(block_weights(shapes[1]))
        own, *weights = pl.pallas_call(
            functools.partial(forward, rank, len(pieces)),
            grid=(steps,),
            in_specs=[
                whole((tokens, rank)),
                block_gated,
                block_message if vectors is not gated else block_first,
            ]
            + [block_weights(piece) for piece in pieces],
            out_specs=specs,
            out_shape=shapes,
            scratch_shapes=[
                pltpu.VMEM((tokens, span), BF16),
                pltpu.VMEM((tokens, width), F32),
                pltpu.VMEM((EXTRA, width), F32),
            ],
            compiler_params=params(),
            cost_estimate=cost,
        )(features, gated, vectors, *pieces)
        return (own, swapped(own)), weights

    def product_shares(weights, *shares):
        return exchanged(
            pl.pallas_call(
                functools.partial(backward, rank, len(shares) == 4),
                grid=(steps,),
                in_specs=[whole((tokens, rank)), block_gated]
                + [whole(partial_shape)] * len(shares)
                + [block_weights(weights)],
                out_specs=block_message,
                out_shape=message_shape,
                scratch_shapes=[pltpu.VMEM((tokens, width), BF16), pltpu.VMEM((8, 128), F32)],
                compiler_params=params(),
                cost_estimate=cost,
            )(features, gated, *shares, weights)
        )

    tail = pl.BlockSpec((TAIL, width), lambda i: (tokens // TAIL, 0))
    full_message = whole(message_shape.shape)
    full_state = whole(state.shape)
    full_alpha = whole((8, units))

    first, (weights,) = mixed_shares(gated, pieces)
    arrived = product_shares(weights, *first)
    message, residual, alpha = pl.pallas_call(
        functools.partial(update, rank),
        grid=(1,),
        in_specs=[SCALAR, SCALAR, full_message, full_state, tail, tail],
        out_specs=[full_message, full_state, full_alpha],
        out_shape=[message_shape, state, jax.ShapeDtypeStruct((8, units), F32)],
        compiler_params=params(),
    )(live, damping, arrived, target, *first)
    second, _ = mixed_shares(exchanged(message), [weights])
    arrived = product_shares(weights, *second, *first)
    x, left = pl.pallas_call(
        functools.partial(finish, rank),
        grid=(1,),
        in_specs=[SCALAR, SCALAR, full_message, full_state] + [tail] * 4 + [full_state, full_alpha],
        out_specs=[full_state, full_state],
        out_shape=[state, state],
        compiler_params=params(),
    )(live, damping, arrived, target, *second, *first, residual, alpha)
    return (x[None], left[None])


def solution(mesh):
    tasks = mesh.shape["task"]
    split = Mesh(mesh.devices.reshape(tasks // 2, 2, 4, 2, 2), ("z", "c", "y", "xa", "xb"))
    task = ("z", "c")
    return jax.shard_map(
        shards,
        mesh=split,
        in_specs=(
            P(task, None, None),
            P(task, None, None),
            P(task, None, ALL),
            P(task),
            P(task),
            P(ALL, task),
            P(task, None, ALL),
        ),
        out_specs=(P(task, None, ALL), P(task, None, ALL)),
        check_vma=False,
    )
```

```python
import functools

import jax
import jax.numpy as jnp
from jax import lax
from jax.experimental import pallas as pl
from jax.experimental.pallas import tpu as pltpu
from jax.sharding import Mesh
from jax.sharding import PartitionSpec as P

F32, BF16 = jnp.float32, jnp.bfloat16
HALF = ("y", "xb")
ROW = ("xa", "xb")
ALL = ("y", "xa", "xb")
EXTRA = 8
TAIL = 16
LATER = 56
TOGETHER = 2


def product(a, b, dims):
    return lax.dot_general(a, b, (dims, ((), ())), preferred_element_type=F32)


def in_pieces(values, shape):
    row = lax.broadcasted_iota(jnp.int32, shape, 0)
    out, at = jnp.zeros(shape, F32), 0
    for value in values:
        rest = jnp.broadcast_to(value, shape)
        for _ in range(3):
            piece = rest.astype(BF16).astype(F32)
            out = jnp.where(row == at, piece, out)
            rest = rest - piece
            at += 1
    return out.astype(BF16)


def from_pieces(rows, at):
    return rows[at : at + 1] + rows[at + 1 : at + 2] + rows[at + 2 : at + 3]


def everywhere(value, shape):
    return jnp.broadcast_to(value[:, :1], shape)


def total(array):
    return jnp.sum(jnp.sum(array, axis=0, keepdims=True), axis=1, keepdims=True)


def post(message, body, scalars, rank):
    pieces = in_pieces(scalars, (EXTRA, body.shape[1]))
    for j in range(message.shape[0]):
        message[j, :rank, :] = body
        message[j, rank:, :] = pieces


def pack(live, gate, grad, message, held):
    tokens = gate.shape[0]
    rank = grad.shape[0]

    @pl.when(pl.program_id(0) == 0)
    def _():
        v = gate[...].astype(F32)
        row = lax.broadcasted_iota(jnp.int32, v.shape, 0)
        held[:tokens, :] = jnp.where(row < live[0], v / (1.0 + jnp.exp(-v)), 0.0).astype(BF16)
        g = grad[...]
        held[tokens : tokens + rank, :] = g.astype(BF16)
        held[tokens + rank :, :] = in_pieces([total(g * g)], (held.shape[0] - tokens - rank, g.shape[1]))

    message[0] = held[...]


def forward(rank, count, features, gated, vectors, *refs):
    pieces, (partial, *outs) = refs[:count], refs[count:]
    if count > 1:
        weights, active, acc, scalars = outs
        at = 0
        for piece in pieces:
            weights[at : at + piece.shape[0], :] = piece[...]
            at += piece.shape[0]
    else:
        (weights,), (active, acc, scalars) = pieces, outs
    step = pl.program_id(0)
    tokens = features.shape[0]
    units = gated.shape[2]

    @pl.when(step == 0)
    def _():
        acc[...] = jnp.zeros_like(acc)
        scalars[...] = jnp.zeros_like(scalars)

    for j in range(gated.shape[0]):
        inner = product(features[...], vectors[j, :rank, :], ((1,), (0,)))
        at = slice(j * units, (j + 1) * units)
        active[:, at] = (gated[j].astype(F32) * inner).astype(BF16)
        scalars[...] += vectors[j, rank : rank + EXTRA, : scalars.shape[1]].astype(F32)
    acc[...] += product(active[...], weights[...], ((1,), (1,)))

    @pl.when(step == pl.num_programs(0) - 1)
    def _():
        partial[:tokens, :] = acc[...].astype(BF16)
        rows = scalars[...]
        partial[tokens:, :] = in_pieces(
            [from_pieces(rows, 0), from_pieces(rows, 3)], (TAIL, rows.shape[1])
        )


def backward(rank, second_pass, features, gated, own, other, *refs):
    before, refs = (refs[0], refs[1:]) if second_pass else (None, refs)
    weights, message, kept, mixed, norm = refs
    step = pl.program_id(0)
    tokens = features.shape[0]

    @pl.when(step == 0)
    def _():
        value = own[:tokens, :].astype(F32) + other[:tokens, :].astype(F32)
        rows = own[tokens:, :].astype(F32) + other[tokens:, :].astype(F32)
        if second_pass:
            kept[...] = rows
            ratio = from_pieces(rows, 0)[:, :1] / from_pieces(before[tokens:, :], 0)[:, :1]
            value = value + everywhere(ratio, value.shape) * before[:tokens, :]
        else:
            kept[:tokens, :] = value
            kept[tokens:, :] = rows
        rounded = value.astype(BF16)
        mixed[...] = rounded
        norm[...] = jnp.broadcast_to(total(value * rounded.astype(F32)), norm.shape)

    units = gated.shape[2]
    pieces = in_pieces([norm[:1, :1]], (EXTRA, units))
    for j in range(gated.shape[0]):
        back = product(mixed[...], weights[:, j * units : (j + 1) * units], ((1,), (0,)))
        second = (gated[j].astype(F32) * back).astype(BF16)
        message[j, :rank, :] = product(features[...], second, ((0,), (0,))).astype(BF16)
        message[j, rank:, :] = pieces


def update(rank, live, rate, arrived, grad, tail, message, residual, alpha):
    rows = arrived[0].astype(F32)
    for j in range(1, arrived.shape[0]):
        rows = rows + arrived[j].astype(F32)
    g = grad[...]
    shape = (1, g.shape[1])
    norm = everywhere(from_pieces(tail[...], 0), shape)
    step = norm / (from_pieces(rows[rank:], 0) / live[0] + rate[0] * norm)
    h = rows[:rank] / live[0] + rate[0] * g
    r = g - step * h
    residual[...] = r
    alpha[...] = jnp.broadcast_to(step, alpha.shape)
    post(message, r.astype(BF16), [total(r * r), total(r * g)], rank)


def finish(rank, live, rate, arrived, grad, tail, tail_was, residual, alpha, x, left):
    rows = arrived[0].astype(F32)
    for j in range(1, arrived.shape[0]):
        rows = rows + arrived[j].astype(F32)
    g, r = grad[...], residual[...]
    shape = (1, g.shape[1])
    norm = everywhere(from_pieces(tail[...], 0), shape)
    cross = everywhere(from_pieces(tail[...], 3), shape)
    norm_was = everywhere(from_pieces(tail_was[...], 0), shape)
    ratio = norm / norm_was
    length = norm + ratio * (2.0 * cross + ratio * norm_was)
    step = norm / (from_pieces(rows[rank:], 0) / live[0] + rate[0] * length)
    d = r + ratio * g
    h = rows[:rank] / live[0] + rate[0] * d
    x[...] = alpha[:1, :] * g + step * d
    left[...] = r - step * h


def whole(array_shape):
    return pl.BlockSpec(array_shape, lambda *_: (0,) * len(array_shape))


SCALAR = pl.BlockSpec(memory_space=pltpu.SMEM)


def params(mebibytes=56):
    return pltpu.CompilerParams(vmem_limit_bytes=mebibytes << 20)


def swapped(array):
    return lax.ppermute(array, ROW, [(0, 3), (3, 0), (1, 2), (2, 1)])


def exchanged(array):
    return lax.all_to_all(array, HALF, split_axis=0, concat_axis=0, tiled=True)


def shifted(array, by):
    size = lax.axis_size("z")
    return lax.ppermute(array, "z", [(i, (i + by) % size) for i in range(size)])


def other_core(array):
    return lax.ppermute(array, "c", [(0, 1), (1, 0)])


def width_block(down_w):
    members = lax.axis_size(HALF)
    units, columns = down_w.shape
    share = columns // members
    padded = -(-share // 16) * 16
    pieces = down_w.T.reshape(members // 2, 2, share, units)
    pieces = jnp.where(lax.axis_index("xa") == 1, pieces[:, ::-1], pieces)
    pieces = jnp.pad(pieces.reshape(members, share, units), ((0, 0), (0, padded - share), (0, 0)))
    mine = exchanged(pieces)
    return jnp.swapaxes(mine, 0, 1).reshape(padded, members * units)


def start_blocks(mine):
    return jnp.concatenate([mine, shifted(mine, 5), shifted(mine, -5)], axis=0)


def all_blocks(near):
    rows = near.shape[0] // 3
    up, down = shifted(near, 1), shifted(near, -1)
    far = jnp.where(lax.axis_index("c") == 0, up[rows : 2 * rows], down[2 * rows :])
    size = lax.axis_size("z")
    both_ways = [(2 * i, 2 * ((i + 2) % size)) for i in range(size)]
    both_ways += [(2 * i + 1, 2 * ((i - 2) % size) + 1) for i in range(size)]
    last = lax.ppermute(far, ("z", "c"), both_ways)
    up2, down2, last = lax.optimization_barrier((shifted(up, 1), shifted(down, -1), last))
    pieces = [near, up, down, up2, down2, last]
    return pieces + [other_core(piece) for piece in pieces]


def shards(support_x, adapter_a, gate_pre, lengths, damping, down_w, grad_b):
    members = lax.axis_size(HALF)
    tokens, units = gate_pre.shape[1:]
    rank = adapter_a.shape[2]
    target = grad_b[0]
    rows = rank + EXTRA
    block_message = pl.BlockSpec((TOGETHER, rows, units), lambda i: (i, 0, 0))
    block_gated = pl.BlockSpec((TOGETHER, tokens, units), lambda i: (i, 0, 0))
    span = TOGETHER * units
    steps = members // TOGETHER
    message_shape = jax.ShapeDtypeStruct((members, rows, units), BF16)
    state = jax.ShapeDtypeStruct((rank, units), F32)

    first_rows = rank + 4 * EXTRA
    packed_shape = (tokens + first_rows, units)
    packed = pl.pallas_call(
        pack,
        grid=(members,),
        in_specs=[SCALAR, whole((tokens, units)), whole((rank, units))],
        out_specs=pl.BlockSpec((1, *packed_shape), lambda i: (i, 0, 0)),
        out_shape=jax.ShapeDtypeStruct((members, *packed_shape), BF16),
        scratch_shapes=[pltpu.VMEM(packed_shape, BF16)],
        compiler_params=params(),
        cost_estimate=pl.CostEstimate(
            flops=8 * tokens * units,
            bytes_accessed=2 * members * packed_shape[0] * units,
            transcendentals=tokens * units,
        ),
    )(lengths, gate_pre[0], target)
    block_first = pl.BlockSpec((TOGETHER, first_rows, units), lambda i: (i, tokens // first_rows, 0))
    mine = width_block(down_w)
    mine, packed = lax.optimization_barrier((mine, packed))
    gated = exchanged(packed)
    features = jnp.dot(support_x[0], adapter_a[0], preferred_element_type=F32).astype(BF16)
    near, features = lax.optimization_barrier((start_blocks(mine), features))
    pieces = all_blocks(near)
    width = sum(piece.shape[0] for piece in pieces)

    def block_weights(array):
        return pl.BlockSpec((array.shape[0], span), lambda i: (0, i))

    live = lengths.astype(F32)
    flops = 2 * tokens * units * members * (width + rank)
    moved = 2 * units * members * (tokens + width + rows)

    cost = pl.CostEstimate(flops=flops, bytes_accessed=moved, transcendentals=0)

    partial_shape = (tokens + TAIL, width)

    def mixed_shares(vectors, pieces):
        shapes = [jax.ShapeDtypeStruct(partial_shape, BF16)]
        specs = [whole(partial_shape)]
        if len(pieces) > 1:
            shapes.append(jax.ShapeDtypeStruct((width, units * members), BF16))
            specs.append(block_weights(shapes[1]))
        own, *weights = pl.pallas_call(
            functools.partial(forward, rank, len(pieces)),
            grid=(steps,),
            in_specs=[
                whole((tokens, rank)),
                block_gated,
                block_message if vectors is not gated else block_first,
            ]
            + [block_weights(piece) for piece in pieces],
            out_specs=specs,
            out_shape=shapes,
            scratch_shapes=[
                pltpu.VMEM((tokens, span), BF16),
                pltpu.VMEM((tokens, width), F32),
                pltpu.VMEM((EXTRA, width), F32),
            ],
            compiler_params=params(56 if len(pieces) > 1 else LATER),
            cost_estimate=cost,
        )(features, gated, vectors, *pieces)
        return (own, swapped(own)), weights

    def product_shares(weights, own, other, *before):
        kept_shape = (TAIL, width) if before else partial_shape
        message, kept = pl.pallas_call(
            functools.partial(backward, rank, bool(before)),
            grid=(steps,),
            in_specs=[whole((tokens, rank)), block_gated]
            + [whole(partial_shape)] * (2 + len(before))
            + [block_weights(weights)],
            out_specs=[block_message, whole(kept_shape)],
            out_shape=[message_shape, jax.ShapeDtypeStruct(kept_shape, F32)],
            scratch_shapes=[pltpu.VMEM((tokens, width), BF16), pltpu.VMEM((8, 128), F32)],
            compiler_params=params(LATER),
            cost_estimate=cost,
        )(features, gated, own, other, *before, weights)
        return exchanged(message), kept

    tail = pl.BlockSpec((TAIL, width), lambda i: (tokens // TAIL, 0))
    full_message = whole(message_shape.shape)
    full_state = whole(state.shape)
    full_alpha = whole((8, units))

    shares, (weights,) = mixed_shares(gated, pieces)
    arrived, first = product_shares(weights, *shares)
    message, residual, alpha = pl.pallas_call(
        functools.partial(update, rank),
        grid=(1,),
        in_specs=[SCALAR, SCALAR, full_message, full_state, tail],
        out_specs=[full_message, full_state, full_alpha],
        out_shape=[message_shape, state, jax.ShapeDtypeStruct((8, units), F32)],
        compiler_params=params(8),
    )(live, damping, arrived, target, first)
    shares, _ = mixed_shares(exchanged(message), [weights])
    arrived, second = product_shares(weights, *shares, first)
    x, left = pl.pallas_call(
        functools.partial(finish, rank),
        grid=(1,),
        in_specs=[SCALAR, SCALAR, full_message, full_state, whole((TAIL, width)), tail]
        + [full_state, full_alpha],
        out_specs=[full_state, full_state],
        out_shape=[state, state],
        compiler_params=params(8),
    )(live, damping, arrived, target, second, first, residual, alpha)
    return (x[None], left[None])


def solution(mesh):
    tasks = mesh.shape["task"]
    split = Mesh(mesh.devices.reshape(tasks // 2, 2, 4, 2, 2), ("z", "c", "y", "xa", "xb"))
    task = ("z", "c")
    return jax.shard_map(
        shards,
        mesh=split,
        in_specs=(
            P(task, None, None),
            P(task, None, None),
            P(task, None, ALL),
            P(task),
            P(task),
            P(ALL, task),
            P(task, None, ALL),
        ),
        out_specs=(P(task, None, ALL), P(task, None, ALL)),
        check_vma=False,
    )
```

```python
import functools

import jax
import jax.numpy as jnp
from jax import lax
from jax.experimental import pallas as pl
from jax.experimental.pallas import tpu as pltpu
from jax.sharding import Mesh
from jax.sharding import PartitionSpec as P

F32, BF16 = jnp.float32, jnp.bfloat16
HALF = ("y", "xb")
ROW = ("xa", "xb")
ALL = ("y", "xa", "xb")
EXTRA = 8
TAIL = 16
LATER = 56
TOGETHER = 2


def product(a, b, dims):
    return lax.dot_general(a, b, (dims, ((), ())), preferred_element_type=F32)


def in_pieces(values, shape):
    row = lax.broadcasted_iota(jnp.int32, shape, 0)
    out, at = jnp.zeros(shape, F32), 0
    for value in values:
        rest = jnp.broadcast_to(value, shape)
        for _ in range(3):
            piece = rest.astype(BF16).astype(F32)
            out = jnp.where(row == at, piece, out)
            rest = rest - piece
            at += 1
    return out.astype(BF16)


def from_pieces(rows, at):
    return rows[at : at + 1] + rows[at + 1 : at + 2] + rows[at + 2 : at + 3]


def everywhere(value, shape):
    return jnp.broadcast_to(value[:, :1], shape)


def total(array):
    return jnp.sum(jnp.sum(array, axis=0, keepdims=True), axis=1, keepdims=True)


def post(message, body, scalars, rank):
    pieces = in_pieces(scalars, (EXTRA, body.shape[1]))
    for j in range(message.shape[0]):
        message[j, :rank, :] = body
        message[j, rank:, :] = pieces


def pack(live, gate, grad, message, held):
    tokens = gate.shape[0]
    rank = grad.shape[0]

    @pl.when(pl.program_id(0) == 0)
    def _():
        v = gate[...].astype(F32)
        row = lax.broadcasted_iota(jnp.int32, v.shape, 0)
        held[:tokens, :] = jnp.where(row < live[0], v / (1.0 + jnp.exp(-v)), 0.0).astype(BF16)
        g = grad[...]
        held[tokens : tokens + rank, :] = g.astype(BF16)
        held[tokens + rank :, :] = in_pieces([total(g * g)], (held.shape[0] - tokens - rank, g.shape[1]))

    message[0] = held[...]


def forward(rank, count, features, gated, vectors, *refs):
    pieces, (partial, *outs) = refs[:count], refs[count:]
    if count > 1:
        weights, active, acc, scalars = outs
        at = 0
        for piece in pieces:
            weights[at : at + piece.shape[0], :] = piece[...]
            at += piece.shape[0]
    else:
        (weights,), (active, acc, scalars) = pieces, outs
    step = pl.program_id(0)
    tokens = features.shape[0]
    units = gated.shape[2]

    @pl.when(step == 0)
    def _():
        acc[...] = jnp.zeros_like(acc)
        scalars[...] = jnp.zeros_like(scalars)

    for j in range(gated.shape[0]):
        inner = product(features[...], vectors[j, :rank, :], ((1,), (0,)))
        at = slice(j * units, (j + 1) * units)
        active[:, at] = (gated[j].astype(F32) * inner).astype(BF16)
        scalars[...] += vectors[j, rank : rank + EXTRA, : scalars.shape[1]].astype(F32)
    acc[...] += product(active[...], weights[...], ((1,), (1,)))

    @pl.when(step == pl.num_programs(0) - 1)
    def _():
        partial[:tokens, :] = acc[...].astype(BF16)
        rows = scalars[...]
        partial[tokens:, :] = in_pieces(
            [from_pieces(rows, 0), from_pieces(rows, 3)], (TAIL, rows.shape[1])
        )


def backward(rank, second_pass, features, gated, own, other, *refs):
    before, refs = (refs[0], refs[1:]) if second_pass else (None, refs)
    weights, message, kept, mixed, norm = refs
    step = pl.program_id(0)
    tokens = features.shape[0]

    @pl.when(step == 0)
    def _():
        value = own[:tokens, :].astype(F32) + other[:tokens, :].astype(F32)
        rows = own[tokens:, :].astype(F32) + other[tokens:, :].astype(F32)
        if second_pass:
            kept[...] = rows
            ratio = from_pieces(rows, 0)[:, :1] / from_pieces(before[tokens:, :], 0)[:, :1]
            value = value + everywhere(ratio, value.shape) * before[:tokens, :]
        else:
            kept[:tokens, :] = value
            kept[tokens:, :] = rows
        rounded = value.astype(BF16)
        mixed[...] = rounded
        norm[...] = jnp.broadcast_to(total(value * rounded.astype(F32)), norm.shape)

    units = gated.shape[2]
    pieces = in_pieces([norm[:1, :1]], (EXTRA, units))
    for j in range(gated.shape[0]):
        back = product(mixed[...], weights[:, j * units : (j + 1) * units], ((1,), (0,)))
        second = (gated[j].astype(F32) * back).astype(BF16)
        message[j, :rank, :] = product(features[...], second, ((0,), (0,))).astype(BF16)
        message[j, rank:, :] = pieces


def update(rank, live, rate, arrived, grad, tail, message, residual, alpha):
    rows = arrived[0].astype(F32)
    for j in range(1, arrived.shape[0]):
        rows = rows + arrived[j].astype(F32)
    g = grad[...]
    shape = (1, g.shape[1])
    norm = everywhere(from_pieces(tail[...], 0), shape)
    step = norm / (from_pieces(rows[rank:], 0) / live[0] + rate[0] * norm)
    h = rows[:rank] / live[0] + rate[0] * g
    r = g - step * h
    residual[...] = r
    alpha[...] = jnp.broadcast_to(step, alpha.shape)
    post(message, r.astype(BF16), [total(r * r), total(r * g)], rank)


def finish(rank, live, rate, arrived, grad, tail, tail_was, residual, alpha, x, left):
    rows = arrived[0].astype(F32)
    for j in range(1, arrived.shape[0]):
        rows = rows + arrived[j].astype(F32)
    g, r = grad[...], residual[...]
    shape = (1, g.shape[1])
    norm = everywhere(from_pieces(tail[...], 0), shape)
    cross = everywhere(from_pieces(tail[...], 3), shape)
    norm_was = everywhere(from_pieces(tail_was[...], 0), shape)
    ratio = norm / norm_was
    length = norm + ratio * (2.0 * cross + ratio * norm_was)
    step = norm / (from_pieces(rows[rank:], 0) / live[0] + rate[0] * length)
    d = r + ratio * g
    h = rows[:rank] / live[0] + rate[0] * d
    x[...] = alpha[:1, :] * g + step * d
    left[...] = r - step * h


def whole(array_shape):
    return pl.BlockSpec(array_shape, lambda *_: (0,) * len(array_shape))


SCALAR = pl.BlockSpec(memory_space=pltpu.SMEM)


def params(mebibytes=56):
    return pltpu.CompilerParams(vmem_limit_bytes=mebibytes << 20)


def swapped(array):
    return lax.ppermute(array, ROW, [(0, 3), (3, 0), (1, 2), (2, 1)])


def exchanged(array):
    return lax.all_to_all(array, HALF, split_axis=0, concat_axis=0, tiled=True)


def shifted(array, by):
    size = lax.axis_size("z")
    return lax.ppermute(array, "z", [(i, (i + by) % size) for i in range(size)])


def other_core(array):
    return lax.ppermute(array, "c", [(0, 1), (1, 0)])


def width_block(down_w):
    members = lax.axis_size(HALF)
    units, columns = down_w.shape
    share = columns // members
    padded = -(-share // 16) * 16
    pieces = down_w.T.reshape(members // 2, 2, share, units)
    pieces = jnp.where(lax.axis_index("xa") == 1, pieces[:, ::-1], pieces)
    pieces = jnp.pad(pieces.reshape(members, share, units), ((0, 0), (0, padded - share), (0, 0)))
    mine = exchanged(pieces)
    return jnp.swapaxes(mine, 0, 1).reshape(padded, members * units)


def all_blocks(near):
    rows = near.shape[0] // 3
    up, down = shifted(near, 1), shifted(near, -1)
    far = jnp.where(lax.axis_index("c") == 0, up[rows : 2 * rows], down[2 * rows :])
    size = lax.axis_size("z")
    both_ways = [(2 * i, 2 * ((i + 2) % size)) for i in range(size)]
    both_ways += [(2 * i + 1, 2 * ((i - 2) % size) + 1) for i in range(size)]
    last = lax.ppermute(far, ("z", "c"), both_ways)
    up2, down2, last = lax.optimization_barrier((shifted(up, 1), shifted(down, -1), last))
    early = jnp.concatenate([near, up, down], axis=0)
    late = jnp.concatenate([up2, down2, last], axis=0)
    return [early, late, other_core(early), other_core(late)]


def shards(support_x, adapter_a, gate_pre, lengths, damping, down_w, grad_b):
    members = lax.axis_size(HALF)
    tokens, units = gate_pre.shape[1:]
    rank = adapter_a.shape[2]
    target = grad_b[0]
    rows = rank + EXTRA
    block_message = pl.BlockSpec((TOGETHER, rows, units), lambda i: (i, 0, 0))
    block_gated = pl.BlockSpec((TOGETHER, tokens, units), lambda i: (i, 0, 0))
    span = TOGETHER * units
    steps = members // TOGETHER
    message_shape = jax.ShapeDtypeStruct((members, rows, units), BF16)
    state = jax.ShapeDtypeStruct((rank, units), F32)

    first_rows = rank + 4 * EXTRA
    packed_shape = (tokens + first_rows, units)
    packed = pl.pallas_call(
        pack,
        grid=(members,),
        in_specs=[SCALAR, whole((tokens, units)), whole((rank, units))],
        out_specs=pl.BlockSpec((1, *packed_shape), lambda i: (i, 0, 0)),
        out_shape=jax.ShapeDtypeStruct((members, *packed_shape), BF16),
        scratch_shapes=[pltpu.VMEM(packed_shape, BF16)],
        compiler_params=params(),
        cost_estimate=pl.CostEstimate(
            flops=8 * tokens * units,
            bytes_accessed=2 * members * packed_shape[0] * units,
            transcendentals=tokens * units,
        ),
    )(lengths, gate_pre[0], target)
    block_first = pl.BlockSpec((TOGETHER, first_rows, units), lambda i: (i, tokens // first_rows, 0))
    mine = width_block(down_w)
    mine, packed = lax.optimization_barrier((mine, packed))
    gated = exchanged(packed)
    below, above = shifted(mine, 5), shifted(mine, -5)
    features = jnp.dot(support_x[0], adapter_a[0], preferred_element_type=F32).astype(BF16)
    near = jnp.concatenate([mine, below, above], axis=0)
    near, features = lax.optimization_barrier((near, features))
    pieces = all_blocks(near)
    width = sum(piece.shape[0] for piece in pieces)

    def block_weights(array):
        return pl.BlockSpec((array.shape[0], span), lambda i: (0, i))

    live = lengths.astype(F32)
    flops = 2 * tokens * units * members * (width + rank)
    moved = 2 * units * members * (tokens + width + rows)

    cost = pl.CostEstimate(flops=flops, bytes_accessed=moved, transcendentals=0)

    partial_shape = (tokens + TAIL, width)

    def mixed_shares(vectors, pieces):
        shapes = [jax.ShapeDtypeStruct(partial_shape, BF16)]
        specs = [whole(partial_shape)]
        if len(pieces) > 1:
            shapes.append(jax.ShapeDtypeStruct((width, units * members), BF16))
            specs.append(block_weights(shapes[1]))
        own, *weights = pl.pallas_call(
            functools.partial(forward, rank, len(pieces)),
            grid=(steps,),
            in_specs=[
                whole((tokens, rank)),
                block_gated,
                block_message if vectors is not gated else block_first,
            ]
            + [block_weights(piece) for piece in pieces],
            out_specs=specs,
            out_shape=shapes,
            scratch_shapes=[
                pltpu.VMEM((tokens, span), BF16),
                pltpu.VMEM((tokens, width), F32),
                pltpu.VMEM((EXTRA, width), F32),
            ],
            compiler_params=params(56 if len(pieces) > 1 else LATER),
            cost_estimate=cost,
        )(features, gated, vectors, *pieces)
        return (own, swapped(own)), weights

    def product_shares(weights, own, other, *before):
        kept_shape = (TAIL, width) if before else partial_shape
        message, kept = pl.pallas_call(
            functools.partial(backward, rank, bool(before)),
            grid=(steps,),
            in_specs=[whole((tokens, rank)), block_gated]
            + [whole(partial_shape)] * (2 + len(before))
            + [block_weights(weights)],
            out_specs=[block_message, whole(kept_shape)],
            out_shape=[message_shape, jax.ShapeDtypeStruct(kept_shape, F32)],
            scratch_shapes=[pltpu.VMEM((tokens, width), BF16), pltpu.VMEM((8, 128), F32)],
            compiler_params=params(LATER),
            cost_estimate=cost,
        )(features, gated, own, other, *before, weights)
        return exchanged(message), kept

    tail = pl.BlockSpec((TAIL, width), lambda i: (tokens // TAIL, 0))
    full_message = whole(message_shape.shape)
    full_state = whole(state.shape)
    full_alpha = whole((8, units))

    shares, (weights,) = mixed_shares(gated, pieces)
    arrived, first = product_shares(weights, *shares)
    message, residual, alpha = pl.pallas_call(
        functools.partial(update, rank),
        grid=(1,),
        in_specs=[SCALAR, SCALAR, full_message, full_state, tail],
        out_specs=[full_message, full_state, full_alpha],
        out_shape=[message_shape, state, jax.ShapeDtypeStruct((8, units), F32)],
        compiler_params=params(8),
    )(live, damping, arrived, target, first)
    shares, _ = mixed_shares(exchanged(message), [weights])
    arrived, second = product_shares(weights, *shares, first)
    x, left = pl.pallas_call(
        functools.partial(finish, rank),
        grid=(1,),
        in_specs=[SCALAR, SCALAR, full_message, full_state, whole((TAIL, width)), tail]
        + [full_state, full_alpha],
        out_specs=[full_state, full_state],
        out_shape=[state, state],
        compiler_params=params(8),
    )(live, damping, arrived, target, second, first, residual, alpha)
    return (x[None], left[None])


def solution(mesh):
    tasks = mesh.shape["task"]
    split = Mesh(mesh.devices.reshape(tasks // 2, 2, 4, 2, 2), ("z", "c", "y", "xa", "xb"))
    task = ("z", "c")
    return jax.shard_map(
        shards,
        mesh=split,
        in_specs=(
            P(task, None, None),
            P(task, None, None),
            P(task, None, ALL),
            P(task),
            P(task),
            P(ALL, task),
            P(task, None, ALL),
        ),
        out_specs=(P(task, None, ALL), P(task, None, ALL)),
        check_vma=False,
    )
```

```python
import functools

import jax
import jax.numpy as jnp
from jax import lax
from jax.experimental import pallas as pl
from jax.experimental.pallas import tpu as pltpu
from jax.sharding import Mesh
from jax.sharding import PartitionSpec as P

F32, BF16 = jnp.float32, jnp.bfloat16
HALF = ("y", "xb")
ROW = ("xa", "xb")
ALL = ("y", "xa", "xb")
EXTRA = 8
TAIL = 16
FIRST, LATER = 56, 53
TOGETHER = 2


def product(a, b, dims):
    return lax.dot_general(a, b, (dims, ((), ())), preferred_element_type=F32)


def in_pieces(values, shape):
    row = lax.broadcasted_iota(jnp.int32, shape, 0)
    out, at = jnp.zeros(shape, F32), 0
    for value in values:
        rest = jnp.broadcast_to(value, shape)
        for _ in range(3):
            piece = rest.astype(BF16).astype(F32)
            out = jnp.where(row == at, piece, out)
            rest = rest - piece
            at += 1
    return out.astype(BF16)


def from_pieces(rows, at):
    return rows[at : at + 1] + rows[at + 1 : at + 2] + rows[at + 2 : at + 3]


def everywhere(value, shape):
    return jnp.broadcast_to(value[:, :1], shape)


def total(array):
    return jnp.sum(jnp.sum(array, axis=0, keepdims=True), axis=1, keepdims=True)


def post(message, body, scalars, rank):
    pieces = in_pieces(scalars, (EXTRA, body.shape[1]))
    for j in range(message.shape[0]):
        message[j, :rank, :] = body
        message[j, rank:, :] = pieces


def pack(live, gate, grad, message, held):
    tokens = gate.shape[0]
    rank = grad.shape[0]

    @pl.when(pl.program_id(0) == 0)
    def _():
        v = gate[...].astype(F32)
        row = lax.broadcasted_iota(jnp.int32, v.shape, 0)
        held[:tokens, :] = jnp.where(row < live[0], v / (1.0 + jnp.exp(-v)), 0.0).astype(BF16)
        g = grad[...]
        held[tokens : tokens + rank, :] = g.astype(BF16)
        held[tokens + rank :, :] = in_pieces([total(g * g)], (held.shape[0] - tokens - rank, g.shape[1]))

    message[0] = held[...]


def forward(rank, count, features, gated, vectors, *refs):
    pieces, (partial, *outs) = refs[:count], refs[count:]
    if count > 1:
        weights, active, acc, scalars = outs
        at = 0
        for piece in pieces:
            weights[at : at + piece.shape[0], :] = piece[...]
            at += piece.shape[0]
    else:
        (weights,), (active, acc, scalars) = pieces, outs
    step = pl.program_id(0)
    tokens = features.shape[0]
    units = gated.shape[2]

    @pl.when(step == 0)
    def _():
        acc[...] = jnp.zeros_like(acc)
        scalars[...] = jnp.zeros_like(scalars)

    for j in range(gated.shape[0]):
        inner = product(features[...], vectors[j, :rank, :], ((1,), (0,)))
        at = slice(j * units, (j + 1) * units)
        active[:, at] = (gated[j].astype(F32) * inner).astype(BF16)
        scalars[...] += vectors[j, rank : rank + EXTRA, : scalars.shape[1]].astype(F32)
    acc[...] += product(active[...], weights[...], ((1,), (1,)))

    @pl.when(step == pl.num_programs(0) - 1)
    def _():
        partial[:tokens, :] = acc[...].astype(BF16)
        rows = scalars[...]
        partial[tokens:, :] = in_pieces(
            [from_pieces(rows, 0), from_pieces(rows, 3)], (TAIL, rows.shape[1])
        )


def backward(rank, second_pass, features, gated, own, other, *refs):
    if second_pass:
        before, rows_before, *refs = refs
    weights, message, *kept, mixed, norm = refs
    step = pl.program_id(0)
    tokens = features.shape[0]

    @pl.when(step == 0)
    def _():
        value = own[:tokens, :].astype(F32) + other[:tokens, :].astype(F32)
        rows = own[tokens:, :].astype(F32) + other[tokens:, :].astype(F32)
        kept[0][...] = rows
        if second_pass:
            ratio = from_pieces(rows, 0)[:, :1] / from_pieces(rows_before[...], 0)[:, :1]
            value = value + everywhere(ratio, value.shape) * before[...]
        else:
            kept[1][...] = value
        rounded = value.astype(BF16)
        mixed[...] = rounded
        norm[...] = jnp.broadcast_to(total(value * rounded.astype(F32)), norm.shape)

    units = gated.shape[2]
    pieces = in_pieces([norm[:1, :1]], (EXTRA, units))
    for j in range(gated.shape[0]):
        back = product(mixed[...], weights[:, j * units : (j + 1) * units], ((1,), (0,)))
        second = (gated[j].astype(F32) * back).astype(BF16)
        message[j, :rank, :] = product(features[...], second, ((0,), (0,))).astype(BF16)
        message[j, rank:, :] = pieces


def update(rank, live, rate, arrived, grad, tail, message, residual, alpha):
    rows = arrived[0].astype(F32)
    for j in range(1, arrived.shape[0]):
        rows = rows + arrived[j].astype(F32)
    g = grad[...]
    shape = (1, g.shape[1])
    norm = everywhere(from_pieces(tail[...], 0), shape)
    step = norm / (from_pieces(rows[rank:], 0) / live[0] + rate[0] * norm)
    h = rows[:rank] / live[0] + rate[0] * g
    r = g - step * h
    residual[...] = r
    alpha[...] = jnp.broadcast_to(step, alpha.shape)
    post(message, r.astype(BF16), [total(r * r), total(r * g)], rank)


def finish(rank, live, rate, arrived, grad, tail, tail_was, residual, alpha, x, left):
    rows = arrived[0].astype(F32)
    for j in range(1, arrived.shape[0]):
        rows = rows + arrived[j].astype(F32)
    g, r = grad[...], residual[...]
    shape = (1, g.shape[1])
    norm = everywhere(from_pieces(tail[...], 0), shape)
    cross = everywhere(from_pieces(tail[...], 3), shape)
    norm_was = everywhere(from_pieces(tail_was[...], 0), shape)
    ratio = norm / norm_was
    length = norm + ratio * (2.0 * cross + ratio * norm_was)
    step = norm / (from_pieces(rows[rank:], 0) / live[0] + rate[0] * length)
    d = r + ratio * g
    h = rows[:rank] / live[0] + rate[0] * d
    x[...] = alpha[:1, :] * g + step * d
    left[...] = r - step * h


def whole(array_shape):
    return pl.BlockSpec(array_shape, lambda *_: (0,) * len(array_shape))


SCALAR = pl.BlockSpec(memory_space=pltpu.SMEM)


def params(mebibytes=56):
    return pltpu.CompilerParams(vmem_limit_bytes=mebibytes << 20)


def swapped(array):
    return lax.ppermute(array, ROW, [(0, 3), (3, 0), (1, 2), (2, 1)])


def exchanged(array):
    return lax.all_to_all(array, HALF, split_axis=0, concat_axis=0, tiled=True)


def shifted(array, by):
    size = lax.axis_size("z")
    return lax.ppermute(array, "z", [(i, (i + by) % size) for i in range(size)])


def other_core(array):
    return lax.ppermute(array, "c", [(0, 1), (1, 0)])


def width_block(down_w):
    members = lax.axis_size(HALF)
    units, columns = down_w.shape
    share = columns // members
    padded = -(-share // 16) * 16
    pieces = down_w.T.reshape(members // 2, 2, share, units)
    pieces = jnp.where(lax.axis_index("xa") == 1, pieces[:, ::-1], pieces)
    pieces = jnp.pad(pieces.reshape(members, share, units), ((0, 0), (0, padded - share), (0, 0)))
    mine = exchanged(pieces)
    return jnp.swapaxes(mine, 0, 1).reshape(padded, members * units)


def all_blocks(near):
    rows = near.shape[0] // 3
    up, down = shifted(near, 1), shifted(near, -1)
    far = jnp.where(lax.axis_index("c") == 0, up[rows : 2 * rows], down[2 * rows :])
    size = lax.axis_size("z")
    both_ways = [(2 * i, 2 * ((i + 2) % size)) for i in range(size)]
    both_ways += [(2 * i + 1, 2 * ((i - 2) % size) + 1) for i in range(size)]
    last = lax.ppermute(far, ("z", "c"), both_ways)
    up2, down2, last = lax.optimization_barrier((shifted(up, 1), shifted(down, -1), last))
    early = jnp.concatenate([near, up, down], axis=0)
    late = jnp.concatenate([up2, down2, last], axis=0)
    return [early, late, other_core(early), other_core(late)]


def shards(support_x, adapter_a, gate_pre, lengths, damping, down_w, grad_b):
    members = lax.axis_size(HALF)
    tokens, units = gate_pre.shape[1:]
    rank = adapter_a.shape[2]
    target = grad_b[0]
    rows = rank + EXTRA
    block_message = pl.BlockSpec((TOGETHER, rows, units), lambda i: (i, 0, 0))
    block_gated = pl.BlockSpec((TOGETHER, tokens, units), lambda i: (i, 0, 0))
    span = TOGETHER * units
    steps = members // TOGETHER
    message_shape = jax.ShapeDtypeStruct((members, rows, units), BF16)
    state = jax.ShapeDtypeStruct((rank, units), F32)

    first_rows = rank + 4 * EXTRA
    packed_shape = (tokens + first_rows, units)
    packed = pl.pallas_call(
        pack,
        grid=(members,),
        in_specs=[SCALAR, whole((tokens, units)), whole((rank, units))],
        out_specs=pl.BlockSpec((1, *packed_shape), lambda i: (i, 0, 0)),
        out_shape=jax.ShapeDtypeStruct((members, *packed_shape), BF16),
        scratch_shapes=[pltpu.VMEM(packed_shape, BF16)],
        compiler_params=params(),
        cost_estimate=pl.CostEstimate(
            flops=8 * tokens * units,
            bytes_accessed=2 * members * packed_shape[0] * units,
            transcendentals=tokens * units,
        ),
    )(lengths, gate_pre[0], target)
    block_first = pl.BlockSpec((TOGETHER, first_rows, units), lambda i: (i, tokens // first_rows, 0))
    mine = width_block(down_w)
    mine, packed = lax.optimization_barrier((mine, packed))
    gated = exchanged(packed)
    below, above = shifted(mine, 5), shifted(mine, -5)
    features = jnp.dot(support_x[0], adapter_a[0], preferred_element_type=F32).astype(BF16)
    near = jnp.concatenate([mine, below, above], axis=0)
    near, features = lax.optimization_barrier((near, features))
    pieces = all_blocks(near)
    width = sum(piece.shape[0] for piece in pieces)

    def block_weights(array):
        return pl.BlockSpec((array.shape[0], span), lambda i: (0, i))

    live = lengths.astype(F32)
    flops = 2 * tokens * units * members * (width + rank)
    moved = 2 * units * members * (tokens + width + rows)

    cost = pl.CostEstimate(flops=flops, bytes_accessed=moved, transcendentals=0)

    partial_shape = (tokens + TAIL, width)

    def mixed_shares(vectors, pieces):
        shapes = [jax.ShapeDtypeStruct(partial_shape, BF16)]
        specs = [whole(partial_shape)]
        if len(pieces) > 1:
            shapes.append(jax.ShapeDtypeStruct((width, units * members), BF16))
            specs.append(block_weights(shapes[1]))
        own, *weights = pl.pallas_call(
            functools.partial(forward, rank, len(pieces)),
            grid=(steps,),
            in_specs=[
                whole((tokens, rank)),
                block_gated,
                block_message if vectors is not gated else block_first,
            ]
            + [block_weights(piece) for piece in pieces],
            out_specs=specs,
            out_shape=shapes,
            scratch_shapes=[
                pltpu.VMEM((tokens, span), BF16),
                pltpu.VMEM((tokens, width), F32),
                pltpu.VMEM((EXTRA, width), F32),
            ],
            compiler_params=params(FIRST if len(pieces) > 1 else LATER),
            cost_estimate=cost,
        )(features, gated, vectors, *pieces)
        return (own, swapped(own)), weights

    def product_shares(weights, own, other, *before):
        kept = [(TAIL, width)] if before else [(TAIL, width), (tokens, width)]
        message, *kept = pl.pallas_call(
            functools.partial(backward, rank, bool(before)),
            grid=(steps,),
            in_specs=[whole((tokens, rank)), block_gated]
            + [whole(partial_shape)] * 2
            + [whole(array.shape) for array in before]
            + [block_weights(weights)],
            out_specs=[block_message] + [whole(shape) for shape in kept],
            out_shape=[message_shape] + [jax.ShapeDtypeStruct(shape, F32) for shape in kept],
            scratch_shapes=[pltpu.VMEM((tokens, width), BF16), pltpu.VMEM((8, 128), F32)],
            compiler_params=params(LATER),
            cost_estimate=cost,
        )(features, gated, own, other, *before, weights)
        return exchanged(message), *kept

    tail = whole((TAIL, width))
    full_message = whole(message_shape.shape)
    full_state = whole(state.shape)
    full_alpha = whole((8, units))

    shares, (weights,) = mixed_shares(gated, pieces)
    arrived, rows_first, first = product_shares(weights, *shares)
    message, residual, alpha = pl.pallas_call(
        functools.partial(update, rank),
        grid=(1,),
        in_specs=[SCALAR, SCALAR, full_message, full_state, tail],
        out_specs=[full_message, full_state, full_alpha],
        out_shape=[message_shape, state, jax.ShapeDtypeStruct((8, units), F32)],
        compiler_params=params(8),
    )(live, damping, arrived, target, rows_first)
    shares, _ = mixed_shares(exchanged(message), [weights])
    arrived, rows_second = product_shares(weights, *shares, first, rows_first)
    x, left = pl.pallas_call(
        functools.partial(finish, rank),
        grid=(1,),
        in_specs=[SCALAR, SCALAR, full_message, full_state, tail, tail]
        + [full_state, full_alpha],
        out_specs=[full_state, full_state],
        out_shape=[state, state],
        compiler_params=params(8),
    )(live, damping, arrived, target, rows_second, rows_first, residual, alpha)
    return (x[None], left[None])


def solution(mesh):
    tasks = mesh.shape["task"]
    split = Mesh(mesh.devices.reshape(tasks // 2, 2, 4, 2, 2), ("z", "c", "y", "xa", "xb"))
    task = ("z", "c")
    return jax.shard_map(
        shards,
        mesh=split,
        in_specs=(
            P(task, None, None),
            P(task, None, None),
            P(task, None, ALL),
            P(task),
            P(task),
            P(ALL, task),
            P(task, None, ALL),
        ),
        out_specs=(P(task, None, ALL), P(task, None, ALL)),
        check_vma=False,
    )
```

```python
import functools

import jax
import jax.numpy as jnp
from jax import lax
from jax.experimental import pallas as pl
from jax.experimental.pallas import tpu as pltpu
from jax.sharding import Mesh
from jax.sharding import PartitionSpec as P

F32, BF16 = jnp.float32, jnp.bfloat16
HALF = ("y", "xb")
ROW = ("xa", "xb")
ALL = ("y", "xa", "xb")
EXTRA = 8
TAIL = 16
FIRST, LATER = 56, 53
WIDER, TOGETHER = 4, 2
CHUNK = 128


def product(a, b, dims):
    return lax.dot_general(a, b, (dims, ((), ())), preferred_element_type=F32)


def in_pieces(values, shape):
    row = lax.broadcasted_iota(jnp.int32, shape, 0)
    out, at = jnp.zeros(shape, F32), 0
    for value in values:
        rest = jnp.broadcast_to(value, shape)
        for _ in range(3):
            piece = rest.astype(BF16).astype(F32)
            out = jnp.where(row == at, piece, out)
            rest = rest - piece
            at += 1
    return out.astype(BF16)


def from_pieces(rows, at):
    return rows[at : at + 1] + rows[at + 1 : at + 2] + rows[at + 2 : at + 3]


def everywhere(value, shape):
    return jnp.broadcast_to(value[:, :1], shape)


def total(array):
    return jnp.sum(jnp.sum(array, axis=0, keepdims=True), axis=1, keepdims=True)


def post(message, body, scalars, rank):
    pieces = in_pieces(scalars, (EXTRA, body.shape[1]))
    for j in range(message.shape[0]):
        message[j, :rank, :] = body
        message[j, rank:, :] = pieces


def pack(live, gate, grad, message, held):
    tokens = gate.shape[0]
    rank = grad.shape[0]

    @pl.when(pl.program_id(0) == 0)
    def _():
        v = gate[...].astype(F32)
        row = lax.broadcasted_iota(jnp.int32, v.shape, 0)
        held[:tokens, :] = jnp.where(row < live[0], v / (1.0 + jnp.exp(-v)), 0.0).astype(BF16)
        g = grad[...]
        held[tokens : tokens + rank, :] = g.astype(BF16)
        held[tokens + rank :, :] = in_pieces([total(g * g)], (held.shape[0] - tokens - rank, g.shape[1]))

    message[0] = held[...]


def forward(rank, count, features, gated, vectors, *refs):
    pieces, (partial, *outs) = refs[:count], refs[count:]
    if count > 1:
        weights, active, acc, scalars = outs
        at = 0
        for piece in pieces:
            weights[at : at + piece.shape[0], :] = piece[...]
            at += piece.shape[0]
    else:
        (weights,), (active, acc, scalars) = pieces, outs
    step = pl.program_id(0)
    tokens = features.shape[0]
    units = gated.shape[2]

    @pl.when(step == 0)
    def _():
        acc[...] = jnp.zeros_like(acc)
        scalars[...] = jnp.zeros_like(scalars)

    for j in range(gated.shape[0]):
        inner = product(features[...], vectors[j, :rank, :], ((1,), (0,)))
        at = slice(j * units, (j + 1) * units)
        active[:, at] = (gated[j].astype(F32) * inner).astype(BF16)
        scalars[...] += vectors[j, rank : rank + EXTRA, : scalars.shape[1]].astype(F32)
    acc[...] += product(active[...], weights[...], ((1,), (1,)))

    @pl.when(step == pl.num_programs(0) - 1)
    def _():
        partial[:tokens, :] = acc[...].astype(BF16)
        rows = scalars[...]
        partial[tokens:, :] = in_pieces(
            [from_pieces(rows, 0), from_pieces(rows, 3)], (TAIL, rows.shape[1])
        )


def backward(rank, second_pass, features, gated, own, other, *refs):
    if second_pass:
        before, rows_before, *refs = refs
    weights, message, *kept, mixed, second, norm = refs
    step = pl.program_id(0)
    tokens = features.shape[0]

    @pl.when(step == 0)
    def _():
        value = own[:tokens, :].astype(F32) + other[:tokens, :].astype(F32)
        rows = own[tokens:, :].astype(F32) + other[tokens:, :].astype(F32)
        kept[0][...] = rows
        if second_pass:
            ratio = from_pieces(rows, 0)[:, :1] / from_pieces(rows_before[...], 0)[:, :1]
            value = value + everywhere(ratio, value.shape) * before[...]
        else:
            kept[1][...] = value
        rounded = value.astype(BF16)
        mixed[...] = rounded
        norm[...] = jnp.broadcast_to(total(value * rounded.astype(F32)), norm.shape)

    units = gated.shape[2]
    pieces = in_pieces([norm[:1, :1]], (EXTRA, units))
    for j in range(gated.shape[0]):
        at = slice(j * units, (j + 1) * units)
        for row in range(0, tokens, CHUNK):
            part = slice(row, row + CHUNK)
            back = product(mixed[part, :], weights[:, at], ((1,), (0,)))
            second[part, at] = (gated[j, part, :].astype(F32) * back).astype(BF16)
        message[j, :rank, :] = product(features[...], second[:, at], ((0,), (0,))).astype(BF16)
        message[j, rank:, :] = pieces


def update(rank, live, rate, arrived, grad, tail, message, residual, alpha):
    rows = arrived[0].astype(F32)
    for j in range(1, arrived.shape[0]):
        rows = rows + arrived[j].astype(F32)
    g = grad[...]
    shape = (1, g.shape[1])
    norm = everywhere(from_pieces(tail[...], 0), shape)
    step = norm / (from_pieces(rows[rank:], 0) / live[0] + rate[0] * norm)
    h = rows[:rank] / live[0] + rate[0] * g
    r = g - step * h
    residual[...] = r
    alpha[...] = jnp.broadcast_to(step, alpha.shape)
    post(message, r.astype(BF16), [total(r * r), total(r * g)], rank)


def finish(rank, live, rate, arrived, grad, tail, tail_was, residual, alpha, x, left):
    rows = arrived[0].astype(F32)
    for j in range(1, arrived.shape[0]):
        rows = rows + arrived[j].astype(F32)
    g, r = grad[...], residual[...]
    shape = (1, g.shape[1])
    norm = everywhere(from_pieces(tail[...], 0), shape)
    cross = everywhere(from_pieces(tail[...], 3), shape)
    norm_was = everywhere(from_pieces(tail_was[...], 0), shape)
    ratio = norm / norm_was
    length = norm + ratio * (2.0 * cross + ratio * norm_was)
    step = norm / (from_pieces(rows[rank:], 0) / live[0] + rate[0] * length)
    d = r + ratio * g
    h = rows[:rank] / live[0] + rate[0] * d
    x[...] = alpha[:1, :] * g + step * d
    left[...] = r - step * h


def whole(array_shape):
    return pl.BlockSpec(array_shape, lambda *_: (0,) * len(array_shape))


SCALAR = pl.BlockSpec(memory_space=pltpu.SMEM)


def params(mebibytes=56):
    return pltpu.CompilerParams(vmem_limit_bytes=mebibytes << 20)


def swapped(array):
    return lax.ppermute(array, ROW, [(0, 3), (3, 0), (1, 2), (2, 1)])


def exchanged(array):
    return lax.all_to_all(array, HALF, split_axis=0, concat_axis=0, tiled=True)


def shifted(array, by):
    size = lax.axis_size("z")
    return lax.ppermute(array, "z", [(i, (i + by) % size) for i in range(size)])


def other_core(array):
    return lax.ppermute(array, "c", [(0, 1), (1, 0)])


def width_block(down_w):
    members = lax.axis_size(HALF)
    units, columns = down_w.shape
    share = columns // members
    padded = -(-share // 16) * 16
    pieces = down_w.T.reshape(members // 2, 2, share, units)
    pieces = jnp.where(lax.axis_index("xa") == 1, pieces[:, ::-1], pieces)
    pieces = jnp.pad(pieces.reshape(members, share, units), ((0, 0), (0, padded - share), (0, 0)))
    mine = exchanged(pieces)
    return jnp.swapaxes(mine, 0, 1).reshape(padded, members * units)


def all_blocks(near):
    rows = near.shape[0] // 3
    up, down = shifted(near, 1), shifted(near, -1)
    far = jnp.where(lax.axis_index("c") == 0, up[rows : 2 * rows], down[2 * rows :])
    size = lax.axis_size("z")
    both_ways = [(2 * i, 2 * ((i + 2) % size)) for i in range(size)]
    both_ways += [(2 * i + 1, 2 * ((i - 2) % size) + 1) for i in range(size)]
    last = lax.ppermute(far, ("z", "c"), both_ways)
    up2, down2, last = lax.optimization_barrier((shifted(up, 1), shifted(down, -1), last))
    early = jnp.concatenate([near, up, down], axis=0)
    late = jnp.concatenate([up2, down2, last], axis=0)
    return [early, late, other_core(early), other_core(late)]


def shards(support_x, adapter_a, gate_pre, lengths, damping, down_w, grad_b):
    members = lax.axis_size(HALF)
    tokens, units = gate_pre.shape[1:]
    rank = adapter_a.shape[2]
    target = grad_b[0]
    rows = rank + EXTRA

    def blocks(together, count, at=0):
        return pl.BlockSpec((together, count, units), lambda i: (i, at, 0))

    message_shape = jax.ShapeDtypeStruct((members, rows, units), BF16)
    state = jax.ShapeDtypeStruct((rank, units), F32)

    first_rows = rank + 4 * EXTRA
    packed_shape = (tokens + first_rows, units)
    packed = pl.pallas_call(
        pack,
        grid=(members,),
        in_specs=[SCALAR, whole((tokens, units)), whole((rank, units))],
        out_specs=pl.BlockSpec((1, *packed_shape), lambda i: (i, 0, 0)),
        out_shape=jax.ShapeDtypeStruct((members, *packed_shape), BF16),
        scratch_shapes=[pltpu.VMEM(packed_shape, BF16)],
        compiler_params=params(),
        cost_estimate=pl.CostEstimate(
            flops=8 * tokens * units,
            bytes_accessed=2 * members * packed_shape[0] * units,
            transcendentals=tokens * units,
        ),
    )(lengths, gate_pre[0], target)
    mine = width_block(down_w)
    mine, packed = lax.optimization_barrier((mine, packed))
    gated = exchanged(packed)
    below, above = shifted(mine, 5), shifted(mine, -5)
    features = jnp.dot(support_x[0], adapter_a[0], preferred_element_type=F32).astype(BF16)
    near = jnp.concatenate([mine, below, above], axis=0)
    near, features = lax.optimization_barrier((near, features))
    pieces = all_blocks(near)
    width = sum(piece.shape[0] for piece in pieces)

    def block_weights(array, together):
        return pl.BlockSpec((array.shape[0], together * units), lambda i: (0, i))

    live = lengths.astype(F32)
    flops = 2 * tokens * units * members * (width + rank)
    moved = 2 * units * members * (tokens + width + rows)

    cost = pl.CostEstimate(flops=flops, bytes_accessed=moved, transcendentals=0)

    partial_shape = (tokens + TAIL, width)

    def mixed_shares(vectors, pieces):
        shapes = [jax.ShapeDtypeStruct(partial_shape, BF16)]
        specs = [whole(partial_shape)]
        if len(pieces) > 1:
            shapes.append(jax.ShapeDtypeStruct((width, units * members), BF16))
            specs.append(block_weights(shapes[1], WIDER))
        own, *weights = pl.pallas_call(
            functools.partial(forward, rank, len(pieces)),
            grid=(members // WIDER,),
            in_specs=[
                whole((tokens, rank)),
                blocks(WIDER, tokens),
                blocks(WIDER, rows)
                if vectors is not gated
                else blocks(WIDER, first_rows, tokens // first_rows),
            ]
            + [block_weights(piece, WIDER) for piece in pieces],
            out_specs=specs,
            out_shape=shapes,
            scratch_shapes=[
                pltpu.VMEM((tokens, WIDER * units), BF16),
                pltpu.VMEM((tokens, width), F32),
                pltpu.VMEM((EXTRA, width), F32),
            ],
            compiler_params=params(FIRST if len(pieces) > 1 else LATER),
            cost_estimate=cost,
        )(features, gated, vectors, *pieces)
        return (own, swapped(own)), weights

    def product_shares(weights, own, other, *before):
        kept = [(TAIL, width)] if before else [(TAIL, width), (tokens, width)]
        message, *kept = pl.pallas_call(
            functools.partial(backward, rank, bool(before)),
            grid=(members // TOGETHER,),
            in_specs=[whole((tokens, rank)), blocks(TOGETHER, tokens)]
            + [whole(partial_shape)] * 2
            + [whole(array.shape) for array in before]
            + [block_weights(weights, TOGETHER)],
            out_specs=[blocks(TOGETHER, rows)] + [whole(shape) for shape in kept],
            out_shape=[message_shape] + [jax.ShapeDtypeStruct(shape, F32) for shape in kept],
            scratch_shapes=[
                pltpu.VMEM((tokens, width), BF16),
                pltpu.VMEM((tokens, TOGETHER * units), BF16),
                pltpu.VMEM((8, 128), F32),
            ],
            compiler_params=params(LATER),
            cost_estimate=cost,
        )(features, gated, own, other, *before, weights)
        return exchanged(message), *kept

    tail = whole((TAIL, width))
    full_message = whole(message_shape.shape)
    full_state = whole(state.shape)
    full_alpha = whole((8, units))

    shares, (weights,) = mixed_shares(gated, pieces)
    arrived, rows_first, first = product_shares(weights, *shares)
    message, residual, alpha = pl.pallas_call(
        functools.partial(update, rank),
        grid=(1,),
        in_specs=[SCALAR, SCALAR, full_message, full_state, tail],
        out_specs=[full_message, full_state, full_alpha],
        out_shape=[message_shape, state, jax.ShapeDtypeStruct((8, units), F32)],
        compiler_params=params(8),
    )(live, damping, arrived, target, rows_first)
    shares, _ = mixed_shares(exchanged(message), [weights])
    arrived, rows_second = product_shares(weights, *shares, first, rows_first)
    x, left = pl.pallas_call(
        functools.partial(finish, rank),
        grid=(1,),
        in_specs=[SCALAR, SCALAR, full_message, full_state, tail, tail]
        + [full_state, full_alpha],
        out_specs=[full_state, full_state],
        out_shape=[state, state],
        compiler_params=params(8),
    )(live, damping, arrived, target, rows_second, rows_first, residual, alpha)
    return (x[None], left[None])


def solution(mesh):
    tasks = mesh.shape["task"]
    split = Mesh(mesh.devices.reshape(tasks // 2, 2, 4, 2, 2), ("z", "c", "y", "xa", "xb"))
    task = ("z", "c")
    return jax.shard_map(
        shards,
        mesh=split,
        in_specs=(
            P(task, None, None),
            P(task, None, None),
            P(task, None, ALL),
            P(task),
            P(task),
            P(ALL, task),
            P(task, None, ALL),
        ),
        out_specs=(P(task, None, ALL), P(task, None, ALL)),
        check_vma=False,
    )
```

```python
import functools

import jax
import jax.numpy as jnp
from jax import lax
from jax.experimental import pallas as pl
from jax.experimental.pallas import tpu as pltpu
from jax.sharding import Mesh
from jax.sharding import PartitionSpec as P

F32, BF16 = jnp.float32, jnp.bfloat16
HALF = ("y", "xb")
ROW = ("xa", "xb")
ALL = ("y", "xa", "xb")
EXTRA = 8
TAIL = 16
FIRST, LATER = 56, 53
WIDER, TOGETHER = 4, 2
CHUNK = 128


def product(a, b, dims):
    return lax.dot_general(a, b, (dims, ((), ())), preferred_element_type=F32)


def in_pieces(values, shape):
    row = lax.broadcasted_iota(jnp.int32, shape, 0)
    out, at = jnp.zeros(shape, F32), 0
    for value in values:
        rest = jnp.broadcast_to(value, shape)
        for _ in range(3):
            piece = rest.astype(BF16).astype(F32)
            out = jnp.where(row == at, piece, out)
            rest = rest - piece
            at += 1
    return out.astype(BF16)


def from_pieces(rows, at):
    return rows[at : at + 1] + rows[at + 1 : at + 2] + rows[at + 2 : at + 3]


def everywhere(value, shape):
    return jnp.broadcast_to(value[:, :1], shape)


def total(array):
    return jnp.sum(jnp.sum(array, axis=0, keepdims=True), axis=1, keepdims=True)


def post(message, body, scalars, rank):
    pieces = in_pieces(scalars, (EXTRA, body.shape[1]))
    for j in range(message.shape[0]):
        message[j, :rank, :] = body
        message[j, rank:, :] = pieces


def pack(live, gate, grad, message, held):
    tokens = gate.shape[0]
    rank = grad.shape[0]

    @pl.when(pl.program_id(0) == 0)
    def _():
        v = gate[...].astype(F32)
        row = lax.broadcasted_iota(jnp.int32, v.shape, 0)
        held[:tokens, :] = jnp.where(row < live[0], v / (1.0 + jnp.exp(-v)), 0.0).astype(BF16)
        g = grad[...]
        held[tokens : tokens + rank, :] = g.astype(BF16)
        held[tokens + rank :, :] = in_pieces([total(g * g)], (held.shape[0] - tokens - rank, g.shape[1]))

    message[0] = held[...]


def forward(rank, count, features, gated, vectors, *refs):
    pieces, (partial, *outs) = refs[:count], refs[count:]
    if count > 1:
        weights, active, acc, scalars = outs
        at = 0
        for piece in pieces:
            weights[at : at + piece.shape[0], :] = piece[...]
            at += piece.shape[0]
    else:
        (weights,), (active, acc, scalars) = pieces, outs
    step = pl.program_id(0)
    tokens = features.shape[0]
    units = gated.shape[2]

    @pl.when(step == 0)
    def _():
        acc[...] = jnp.zeros_like(acc)
        scalars[...] = jnp.zeros_like(scalars)

    for j in range(gated.shape[0]):
        inner = product(features[...], vectors[j, :rank, :], ((1,), (0,)))
        at = slice(j * units, (j + 1) * units)
        active[:, at] = (gated[j].astype(F32) * inner).astype(BF16)
        scalars[...] += vectors[j, rank : rank + EXTRA, : scalars.shape[1]].astype(F32)
    acc[...] += product(active[...], weights[...], ((1,), (1,)))

    @pl.when(step == pl.num_programs(0) - 1)
    def _():
        partial[:tokens, :] = acc[...].astype(BF16)
        rows = scalars[...]
        partial[tokens:, :] = in_pieces(
            [from_pieces(rows, 0), from_pieces(rows, 3)], (TAIL, rows.shape[1])
        )


def backward(rank, second_pass, features, gated, own, other, *refs):
    if second_pass:
        before, rows_before, *refs = refs
    weights, message, *kept, mixed, second, norm = refs
    step = pl.program_id(0)
    tokens = features.shape[0]

    @pl.when(step == 0)
    def _():
        value = own[:tokens, :].astype(F32) + other[:tokens, :].astype(F32)
        rows = own[tokens:, :].astype(F32) + other[tokens:, :].astype(F32)
        kept[0][...] = rows
        if second_pass:
            ratio = from_pieces(rows, 0)[:, :1] / from_pieces(rows_before[...], 0)[:, :1]
            value = value + everywhere(ratio, value.shape) * before[...]
        else:
            kept[1][...] = value
        rounded = value.astype(BF16)
        mixed[...] = rounded
        norm[...] = jnp.broadcast_to(total(value * rounded.astype(F32)), norm.shape)

    units = gated.shape[2]
    pieces = in_pieces([norm[:1, :1]], (EXTRA, units))
    for j in range(gated.shape[0]):
        at = slice(j * units, (j + 1) * units)
        for row in range(0, tokens, CHUNK):
            part = slice(row, row + CHUNK)
            back = product(mixed[part, :], weights[:, at], ((1,), (0,)))
            second[part, at] = (gated[j, part, :].astype(F32) * back).astype(BF16)
        message[j, :rank, :] = product(features[...], second[:, at], ((0,), (0,))).astype(BF16)
        message[j, rank:, :] = pieces


def update(rank, given, arrived, grad, tail, message, residual, alpha):
    rows = arrived[0].astype(F32)
    for j in range(1, arrived.shape[0]):
        rows = rows + arrived[j].astype(F32)
    g = grad[...]
    shape = (1, g.shape[1])
    norm = everywhere(from_pieces(tail[...], 0), shape)
    step = norm / (from_pieces(rows[rank:], 0) / given[0] + given[1] * norm)
    h = rows[:rank] / given[0] + given[1] * g
    r = g - step * h
    residual[...] = r
    alpha[...] = jnp.broadcast_to(step, alpha.shape)
    post(message, r.astype(BF16), [total(r * r), total(r * g)], rank)


def finish(rank, given, arrived, grad, tail, tail_was, residual, alpha, x, left):
    rows = arrived[0].astype(F32)
    for j in range(1, arrived.shape[0]):
        rows = rows + arrived[j].astype(F32)
    g, r = grad[...], residual[...]
    shape = (1, g.shape[1])
    norm = everywhere(from_pieces(tail[...], 0), shape)
    cross = everywhere(from_pieces(tail[...], 3), shape)
    norm_was = everywhere(from_pieces(tail_was[...], 0), shape)
    ratio = norm / norm_was
    length = norm + ratio * (2.0 * cross + ratio * norm_was)
    step = norm / (from_pieces(rows[rank:], 0) / given[0] + given[1] * length)
    d = r + ratio * g
    h = rows[:rank] / given[0] + given[1] * d
    x[...] = alpha[:1, :] * g + step * d
    left[...] = r - step * h


def whole(array_shape):
    return pl.BlockSpec(array_shape, lambda *_: (0,) * len(array_shape))


SCALAR = pl.BlockSpec(memory_space=pltpu.SMEM)


def params(mebibytes=56):
    return pltpu.CompilerParams(vmem_limit_bytes=mebibytes << 20)


def swapped(array):
    return lax.ppermute(array, ROW, [(0, 3), (3, 0), (1, 2), (2, 1)])


def exchanged(array):
    return lax.all_to_all(array, HALF, split_axis=0, concat_axis=0, tiled=True)


def shifted(array, by):
    size = lax.axis_size("z")
    return lax.ppermute(array, "z", [(i, (i + by) % size) for i in range(size)])


def other_core(array):
    return lax.ppermute(array, "c", [(0, 1), (1, 0)])


def width_block(down_w):
    members = lax.axis_size(HALF)
    units, columns = down_w.shape
    share = columns // members
    padded = -(-share // 16) * 16
    pieces = down_w.T.reshape(members // 2, 2, share, units)
    pieces = jnp.where(lax.axis_index("xa") == 1, pieces[:, ::-1], pieces)
    pieces = jnp.pad(pieces.reshape(members, share, units), ((0, 0), (0, padded - share), (0, 0)))
    mine = exchanged(pieces)
    return jnp.swapaxes(mine, 0, 1).reshape(padded, members * units)


def all_blocks(near):
    rows = near.shape[0] // 3
    up, down = shifted(near, 1), shifted(near, -1)
    far = jnp.where(lax.axis_index("c") == 0, up[rows : 2 * rows], down[2 * rows :])
    size = lax.axis_size("z")
    both_ways = [(2 * i, 2 * ((i + 2) % size)) for i in range(size)]
    both_ways += [(2 * i + 1, 2 * ((i - 2) % size) + 1) for i in range(size)]
    last = lax.ppermute(far, ("z", "c"), both_ways)
    up2, down2, last = lax.optimization_barrier((shifted(up, 1), shifted(down, -1), last))
    early = jnp.concatenate([near, up, down], axis=0)
    late = jnp.concatenate([up2, down2, last], axis=0)
    return [early, late, other_core(early), other_core(late)]


def shards(support_x, adapter_a, gate_pre, lengths, damping, down_w, grad_b):
    members = lax.axis_size(HALF)
    tokens, units = gate_pre.shape[1:]
    rank = adapter_a.shape[2]
    target = grad_b[0]
    rows = rank + EXTRA

    def blocks(together, count, at=0):
        return pl.BlockSpec((together, count, units), lambda i: (i, at, 0))

    message_shape = jax.ShapeDtypeStruct((members, rows, units), BF16)
    state = jax.ShapeDtypeStruct((rank, units), F32)

    first_rows = rank + 4 * EXTRA
    packed_shape = (tokens + first_rows, units)
    packed = pl.pallas_call(
        pack,
        grid=(members,),
        in_specs=[SCALAR, whole((tokens, units)), whole((rank, units))],
        out_specs=pl.BlockSpec((1, *packed_shape), lambda i: (i, 0, 0)),
        out_shape=jax.ShapeDtypeStruct((members, *packed_shape), BF16),
        scratch_shapes=[pltpu.VMEM(packed_shape, BF16)],
        compiler_params=params(),
        cost_estimate=pl.CostEstimate(
            flops=8 * tokens * units,
            bytes_accessed=2 * members * packed_shape[0] * units,
            transcendentals=tokens * units,
        ),
    )(lengths, gate_pre[0], target)
    mine = width_block(down_w)
    mine, packed = lax.optimization_barrier((mine, packed))
    gated = exchanged(packed)
    below, above = shifted(mine, 5), shifted(mine, -5)
    features = jnp.dot(support_x[0], adapter_a[0], preferred_element_type=F32).astype(BF16)
    near = jnp.concatenate([mine, below, above], axis=0)
    scalars = jnp.concatenate([lengths.astype(F32), damping])
    near, features, scalars = lax.optimization_barrier((near, features, scalars))
    pieces = all_blocks(near)
    width = sum(piece.shape[0] for piece in pieces)

    def block_weights(array, together):
        return pl.BlockSpec((array.shape[0], together * units), lambda i: (0, i))

    flops = 2 * tokens * units * members * (width + rank)
    moved = 2 * units * members * (tokens + width + rows)

    cost = pl.CostEstimate(flops=flops, bytes_accessed=moved, transcendentals=0)

    partial_shape = (tokens + TAIL, width)

    def mixed_shares(vectors, pieces):
        shapes = [jax.ShapeDtypeStruct(partial_shape, BF16)]
        specs = [whole(partial_shape)]
        if len(pieces) > 1:
            shapes.append(jax.ShapeDtypeStruct((width, units * members), BF16))
            specs.append(block_weights(shapes[1], WIDER))
        own, *weights = pl.pallas_call(
            functools.partial(forward, rank, len(pieces)),
            grid=(members // WIDER,),
            in_specs=[
                whole((tokens, rank)),
                blocks(WIDER, tokens),
                blocks(WIDER, rows)
                if vectors is not gated
                else blocks(WIDER, first_rows, tokens // first_rows),
            ]
            + [block_weights(piece, WIDER) for piece in pieces],
            out_specs=specs,
            out_shape=shapes,
            scratch_shapes=[
                pltpu.VMEM((tokens, WIDER * units), BF16),
                pltpu.VMEM((tokens, width), F32),
                pltpu.VMEM((EXTRA, width), F32),
            ],
            compiler_params=params(FIRST if len(pieces) > 1 else LATER),
            cost_estimate=cost,
        )(features, gated, vectors, *pieces)
        return (own, swapped(own)), weights

    def product_shares(weights, own, other, *before):
        kept = [(TAIL, width)] if before else [(TAIL, width), (tokens, width)]
        message, *kept = pl.pallas_call(
            functools.partial(backward, rank, bool(before)),
            grid=(members // TOGETHER,),
            in_specs=[whole((tokens, rank)), blocks(TOGETHER, tokens)]
            + [whole(partial_shape)] * 2
            + [whole(array.shape) for array in before]
            + [block_weights(weights, TOGETHER)],
            out_specs=[blocks(TOGETHER, rows)] + [whole(shape) for shape in kept],
            out_shape=[message_shape] + [jax.ShapeDtypeStruct(shape, F32) for shape in kept],
            scratch_shapes=[
                pltpu.VMEM((tokens, width), BF16),
                pltpu.VMEM((tokens, TOGETHER * units), BF16),
                pltpu.VMEM((8, 128), F32),
            ],
            compiler_params=params(LATER),
            cost_estimate=cost,
        )(features, gated, own, other, *before, weights)
        return exchanged(message), *kept

    tail = whole((TAIL, width))
    full_message = whole(message_shape.shape)
    full_state = whole(state.shape)
    full_alpha = whole((8, units))

    shares, (weights,) = mixed_shares(gated, pieces)
    arrived, rows_first, first = product_shares(weights, *shares)
    message, residual, alpha = pl.pallas_call(
        functools.partial(update, rank),
        grid=(1,),
        in_specs=[SCALAR, full_message, full_state, tail],
        out_specs=[full_message, full_state, full_alpha],
        out_shape=[message_shape, state, jax.ShapeDtypeStruct((8, units), F32)],
        compiler_params=params(8),
    )(scalars, arrived, target, rows_first)
    shares, _ = mixed_shares(exchanged(message), [weights])
    arrived, rows_second = product_shares(weights, *shares, first, rows_first)
    x, left = pl.pallas_call(
        functools.partial(finish, rank),
        grid=(1,),
        in_specs=[SCALAR, full_message, full_state, tail, tail]
        + [full_state, full_alpha],
        out_specs=[full_state, full_state],
        out_shape=[state, state],
        compiler_params=params(8),
    )(scalars, arrived, target, rows_second, rows_first, residual, alpha)
    return (x[None], left[None])


def solution(mesh):
    tasks = mesh.shape["task"]
    split = Mesh(mesh.devices.reshape(tasks // 2, 2, 4, 2, 2), ("z", "c", "y", "xa", "xb"))
    task = ("z", "c")
    return jax.shard_map(
        shards,
        mesh=split,
        in_specs=(
            P(task, None, None),
            P(task, None, None),
            P(task, None, ALL),
            P(task),
            P(task),
            P(ALL, task),
            P(task, None, ALL),
        ),
        out_specs=(P(task, None, ALL), P(task, None, ALL)),
        check_vma=False,
    )
```
